256 devices in a mesh: ctx: 32 (over x, y, core), head: 8 (over z).
Axes of the slice: x: 4, y: 4, z: 8, core: 2. Of those that a mesh axis runs over, the one named last changes fastest.
Arguments:
- queries: bfloat16 [8192, 4096], P('ctx', 'head'), may hold values from -6 to 6
- keys: bfloat16 [8192, 2, 4096], P('ctx', None, 'head'), may hold values from -6 to 6
- values: bfloat16 [8192, 2, 4096], P('ctx', None, 'head'), may hold values from -6 to 6
- beta: float32 [32, 2, 8192], P('head', None, 'ctx'), as said below
- log_gate: float32 [32, 8192], P('head', 'ctx'), as said below
- norm_gain: float32 [4096], P('head'), may hold values from 0.1 to 1.9
- out_weight: bfloat16 [4096, 4096], P('head'), may hold values from -0.09375 to 0.09375
Outputs:
- mixed: bfloat16 [8192, 4096], P(('ctx', 'head'))
The draws below stay inside these ranges and needn't reach their ends.
Inputs may be any that keep to these rules, and one draw needn't show every extreme that they name: `beta`: strictly below 2. `log_gate`: never positive.
All inputs are finite; a program needn't handle non-finite values.
Results may differ from the reference program's by a relative error of at most 0.025.
Values may be sent and summed in bfloat16 or wider, within the bound.
No kernel may reach another device: no remote copies, remote signals or barrier semaphores. Data moves between devices by JAX's collectives and lax.ppermute only.
A program may use at most 128 MiB of HBM per device.

```python
import jax
import jax.numpy as jnp
from jax import lax

D = 4096
DH = 128
HEAD_DEV = 4
CT = 32
HEAD_TOTAL = 32
TOKEN_TOTAL = 8192
N_HEAD = 8


def slow_heads(key):
    chosen = jax.random.uniform(jax.random.fold_in(key, 11), (HEAD_TOTAL,), jnp.float32)
    slow_share = 0.5
    return chosen < slow_share


def rough_factor(key, shape):
    return jnp.exp(jax.random.uniform(key, shape, jnp.float32, jnp.log(0.5), jnp.log(2.0)))


def draw_beta(key, part):
    slow_mask = slow_heads(key)[:, None, None]
    first_key, second_key, extra_random_key = jax.random.split(jax.random.fold_in(key, 21), 3)
    margin = jnp.exp(jax.random.uniform(first_key, (HEAD_TOTAL, 1, 1), jnp.float32, jnp.log(0.03), jnp.log(0.25))) * DH / (2.0 * TOKEN_TOTAL)
    slow_beta = 2.0 - margin * rough_factor(second_key, (HEAD_TOTAL, 2, TOKEN_TOTAL))
    fast_beta = jax.random.uniform(extra_random_key, (HEAD_TOTAL, 2, TOKEN_TOTAL), jnp.float32, 0.1, 1.9)
    return jnp.where(slow_mask, slow_beta, fast_beta)


def draw_log_gate(key, part):
    slow_mask = slow_heads(key)[:, None]
    first_key, second_key, extra_random_key, fourth_key = jax.random.split(jax.random.fold_in(key, 31), 4)
    fast_rate = jnp.exp(jax.random.uniform(first_key, (HEAD_TOTAL, 1), jnp.float32, jnp.log(1.0 / 50.0), jnp.log(1.0 / 15.0)))
    head_rate = jnp.where(slow_mask, 0.2 / TOKEN_TOTAL, fast_rate)
    baseline_log_gates = -head_rate * rough_factor(second_key, (HEAD_TOTAL, TOKEN_TOTAL))
    token_span_width = jax.random.uniform(extra_random_key, (HEAD_TOTAL, TOKEN_TOTAL), jnp.float32) < 2.0 / TOKEN_TOTAL
    decay_log_terms = jnp.log(jax.random.uniform(fourth_key, (HEAD_TOTAL, TOKEN_TOTAL), jnp.float32, 0.5, 0.8))
    return baseline_log_gates + jnp.where(token_span_width, decay_log_terms, 0.0)


def shard_levels(key, shape, cuts, low, largest):
    loudness, own = 1.0, jax.random.fold_in(key, 6)
    for axis_at, blocks in cuts:
        steps = jnp.exp(jax.random.uniform(jax.random.fold_in(own, axis_at), (blocks,), jnp.float32, low / len(cuts), largest / len(cuts)))
        loudness = loudness * jnp.repeat(steps, shape[axis_at] // blocks).reshape([-1 if axis == axis_at else 1 for axis in range(len(shape))])
    return loudness


def centred(stream_key, dims, deviation, reach, cuts=(), kind=jnp.bfloat16):
    result = jax.random.normal(stream_key, dims, jnp.float32) * deviation
    if len(cuts) > 0:
        result = shard_levels(stream_key, dims, cuts, -0.22, 0.18) * result
    return jnp.clip(result, min=-reach, max=reach).astype(kind)


def setup_inputs(seed: int = 0) -> dict:
    key_list = jax.random.split(jax.random.key(seed), 8)
    queries = centred(key_list[0], (TOKEN_TOTAL, HEAD_TOTAL * DH), 1.0, 6.0, ((0, 32), (1, 8)))
    keys = centred(key_list[1], (TOKEN_TOTAL, 2, HEAD_TOTAL * DH), 1.0, 6.0, ((0, 32), (2, 8)))
    values = centred(key_list[2], (TOKEN_TOTAL, 2, HEAD_TOTAL * DH), 1.0, 6.0, ((0, 32), (2, 8)))
    beta = draw_beta(jax.random.fold_in(key_list[7], 71), 0)
    log_gate = draw_log_gate(jax.random.fold_in(key_list[7], 71), 0)
    norm_gain = jnp.clip(1.0 + 0.18 * jax.random.normal(key_list[5], (HEAD_TOTAL * DH,), jnp.float32), 0.1, 1.9)
    out_weight = centred(key_list[6], (HEAD_TOTAL * DH, D), (HEAD_TOTAL * DH) ** -0.5, 0.09375, ((0, 8),))
    return dict(queries=queries, keys=keys, values=values, beta=beta, log_gate=log_gate, norm_gain=norm_gain, out_weight=out_weight)


highest = lax.Precision.HIGHEST

def normalize(key_rows):
    return key_rows * lax.rsqrt(lax.optimization_barrier(jnp.sum(key_rows * key_rows, axis=-1, keepdims=True)) + 1e-06)

def span_terms(query_rows, key_rows, value_rows, beta_values_rows, gate_rows):
    step_count = key_rows.shape[-2]
    cumulative = jnp.cumsum(gate_rows, axis=-1)
    later_step = jnp.arange(step_count)[:, None]
    earlier_step = jnp.arange(step_count)[None, :]
    strict = later_step > earlier_step
    gap_logs = cumulative[..., :, None] - cumulative[..., None, :]
    decay_ratio = jnp.where(strict, jnp.exp(jnp.where(strict, gap_logs, 0.0)), 0.0)
    key_inner = jnp.einsum('...sd,...rd->...sr', key_rows, key_rows, precision=highest)
    lower_part = decay_ratio * beta_values_rows[..., None, :] * key_inner
    system = jnp.eye(step_count, dtype=key_rows.dtype) + lower_part
    right_side = jnp.concatenate([value_rows, jnp.exp(cumulative)[..., None] * key_rows], axis=-1)
    solved = lax.linalg.triangular_solve(system, right_side, left_side=True, lower=True, unit_diagonal=True)
    value_width = value_rows.shape[-1]
    fresh_values = solved[..., :value_width]
    carried = solved[..., value_width:]
    span_total = cumulative[..., -1]
    scaled = (jnp.exp(span_total[..., None] - cumulative) * beta_values_rows)[..., None] * key_rows
    identity_key = jnp.eye(key_rows.shape[-1], dtype=key_rows.dtype)
    transition = jnp.exp(span_total)[..., None, None] * identity_key - jnp.einsum('...rd,...re->...de', scaled, carried, precision=highest)
    offset = jnp.einsum('...rd,...re->...de', scaled, fresh_values, precision=highest)
    read_logs = cumulative[..., 1::2]
    row_index = jnp.arange(query_rows.shape[-2])[:, None]
    visible = 2 * row_index + 1 >= earlier_step
    read_gaps = read_logs[..., :, None] - cumulative[..., None, :]
    weight = jnp.where(visible, jnp.exp(jnp.where(visible, read_gaps, 0.0)), 0.0)
    scores = jnp.einsum('...td,...rd->...tr', query_rows, key_rows, precision=highest) * weight * beta_values_rows[..., None, :]
    lead_rows = jnp.exp(read_logs)[..., None] * query_rows - jnp.einsum('...tr,...re->...te', scores, carried, precision=highest)
    local_part = jnp.einsum('...tr,...re->...te', scores, fresh_values, precision=highest)
    return (transition, offset, lead_rows, local_part)

def reference(queries, keys, values, beta, log_gate, norm_gain, out_weight):
    spans = TOKEN_TOTAL // CT
    query_all = queries.reshape(spans, CT, HEAD_TOTAL, DH)
    key_all = keys.reshape(spans, CT, 2, HEAD_TOTAL, DH).reshape(spans, 2 * CT, HEAD_TOTAL, DH)
    value_all = values.reshape(spans, CT, 2, HEAD_TOTAL, DH).reshape(spans, 2 * CT, HEAD_TOTAL, DH)
    beta_all = jnp.transpose(beta, (2, 1, 0)).reshape(spans, 2 * CT, HEAD_TOTAL)
    gate_pair = jnp.stack([log_gate.T, jnp.zeros_like(log_gate.T)], axis=1)
    gate_all = gate_pair.reshape(spans, 2 * CT, HEAD_TOTAL)
    head_gain = norm_gain.reshape(HEAD_TOTAL, 1, DH)

    def advance(memory, inputs):
        query_block, key_block, value_block, beta_block, gate_block = inputs
        query_rows = jnp.swapaxes(query_block.astype(jnp.float32), 0, 1)
        key_rows = normalize(jnp.swapaxes(key_block.astype(jnp.float32), 0, 1))
        value_rows = jnp.swapaxes(value_block.astype(jnp.float32), 0, 1)
        transition, offset, lead_rows, local_part = span_terms(query_rows, key_rows, value_rows, beta_block.T, gate_block.T)
        read_rows = jnp.einsum('htd,hde->hte', lead_rows, memory, precision=highest) + local_part
        row_scale = lax.rsqrt(lax.optimization_barrier(jnp.mean(read_rows * read_rows, axis=-1, keepdims=True)) + 1e-06)
        normed = read_rows * row_scale * head_gain
        out_rows = jnp.swapaxes(normed, 0, 1).reshape(CT, HEAD_TOTAL * DH).astype(jnp.bfloat16)
        updated = jnp.einsum('hde,hef->hdf', transition, memory, precision=highest) + offset
        return (updated, out_rows)
    start_memory = jnp.zeros((HEAD_TOTAL, DH, DH), jnp.float32)
    _, blocks = lax.scan(advance, start_memory, (query_all, key_all, value_all, beta_all, gate_all))
    flat_rows = blocks.reshape(TOKEN_TOTAL, HEAD_TOTAL * DH)
    group_width = HEAD_DEV * DH
    summed = jnp.zeros((TOKEN_TOTAL, D), jnp.float32)
    for group_index in range(N_HEAD):
        low = group_index * group_width
        partial_value = jnp.dot(flat_rows[:, low:low + group_width].astype(jnp.float32), out_weight[low:low + group_width].astype(jnp.float32), preferred_element_type=jnp.float32).astype(jnp.bfloat16)
        summed = summed + partial_value.astype(jnp.float32)
    return summed.astype(jnp.bfloat16)
```

```python
import functools

import jax
import jax.numpy as jnp
from jax import lax
from jax.experimental import pallas as pl
from jax.experimental.pallas import tpu as pltpu
from jax.sharding import PartitionSpec as P

DH = 128
STEPS = 128
ROWS = STEPS // 2
F32 = jnp.float32
BF16 = jnp.bfloat16
NN = (((1,), (0,)), ((), ()))
NT = (((1,), (1,)), ((), ()))
TN = (((0,), (0,)), ((), ()))
VMEM = pl.BlockSpec(memory_space=pltpu.VMEM)
SMEM = pl.BlockSpec(memory_space=pltpu.SMEM)


def dot(a, b, dims=NN):
    return lax.dot_general(a, b, dims, preferred_element_type=F32)


def split(x):
    high = x.astype(BF16)
    return high, (x - high.astype(F32)).astype(BF16)


def dot_wide(a, b, dims=NN):
    a_high, a_low = split(a)
    b_high, b_low = split(b)
    return dot(a_high, b_high, dims) + (dot(a_high, b_low, dims) + dot(a_low, b_high, dims))


def dot_left(a, b, dims=NN):
    high, low = split(a)
    return dot(high, b, dims) + dot(low, b, dims)


def dot_right(a, b, dims=NN):
    high, low = split(b)
    return dot(a, high, dims) + dot(a, low, dims)


def iotas(rows, columns):
    return (
        lax.broadcasted_iota(jnp.int32, (rows, columns), 0),
        lax.broadcasted_iota(jnp.int32, (rows, columns), 1),
    )


def gate_sums(gates, betas):
    token, step = iotas(ROWS, STEPS)
    high = lax.Precision.HIGHEST
    upto = (2 * token <= step).astype(F32)
    sums = jnp.dot(gates, upto, precision=high, preferred_element_type=F32)
    even = (2 * token == step).astype(F32)
    odd = (2 * token + 1 == step).astype(F32)
    spread = jnp.dot(betas[0], even, precision=high, preferred_element_type=F32) + jnp.dot(
        betas[1], odd, precision=high, preferred_element_type=F32
    )
    return sums, spread


def unit_inverses(lowers):
    row, column = iotas(STEPS, STEPS)
    eye = (row == column).astype(F32)
    pairs = (row // 2 == column // 2) & (row > column)
    inverses = [eye - jnp.where(pairs, lower, 0.0) for lower in lowers]
    size = 2
    while size < STEPS:
        corner = (row // (2 * size) == column // (2 * size)) & (row // size > column // size)
        corners = [jnp.where(corner, lower, 0.0) for lower in lowers]
        parts = [split(inverse) for inverse in inverses]
        rights = [
            dot_right_parts(split(block), part) for block, part in zip(corners, parts)
        ]
        inverses = [
            inverse - dot_right_parts(part, split(right))
            for inverse, part, right in zip(inverses, parts, rights)
        ]
        size *= 2
    return inverses


def dot_right_parts(a, b):
    return dot(a[0], b[0]) + (dot(a[0], b[1]) + dot(a[1], b[0]))


def local_kernel(
    heads, chunks, place_ref, k_ref, v_ref, beta_ref, gate_ref,
    mine_ref, theirs_ref, solved_ref, before_ref, rows_ref,
):
    core = place_ref[0]
    keys_all = k_ref.reshape(2 * k_ref.shape[0], k_ref.shape[2])
    values_all = v_ref.reshape(2 * v_ref.shape[0], v_ref.shape[2])
    row, column = iotas(STEPS, STEPS)
    eye = row == column
    strict = row > column

    def down(line):
        return jnp.sum(jnp.where(eye, line, 0.0), axis=1, keepdims=True)

    def across(stack):
        return jnp.sum(jnp.where(eye, stack, 0.0), axis=0, keepdims=True)

    work = []
    for c in range(chunks):
        at = pl.ds(c * ROWS, ROWS)
        gates = jnp.maximum(gate_ref[:, at], -200.0)
        sums, spread = gate_sums(gates, (beta_ref[:, 0, at], beta_ref[:, 1, at]))
        for h in range(heads):
            key = keys_all[pl.ds(c * STEPS, STEPS), pl.ds(h * DH, DH)]
            wide = key.astype(F32)
            norm = lax.rsqrt(jnp.sum(wide * wide, axis=1, keepdims=True) + 1e-06)
            norm_line = across(norm)
            total = sums[h : h + 1]
            total_down = down(total)
            beta_line = spread[h : h + 1]
            inner = dot(key, key, NT)
            decay = jnp.exp(jnp.minimum(total_down - total, 0.0))
            lower = jnp.where(strict, decay * (inner * norm) * (norm_line * beta_line), 0.0)
            rows_ref[h, c] = jnp.concatenate(
                [total, beta_line * norm_line, jnp.zeros((6, STEPS), F32)], axis=0
            )
            last = total[:, STEPS - 1 :]
            scale = jnp.exp(jnp.minimum(last - total_down, 0.0)) * down(beta_line) * norm
            work.append((c, h, key, lower, jnp.exp(total) * norm_line, scale, jnp.exp(last)))
    inverses = unit_inverses([w[3] for w in work])
    maps = {}
    for (c, h, key, _, carry, scale, fade), inverse in zip(work, inverses):
        value = values_all[pl.ds(c * STEPS, STEPS), pl.ds(h * DH, DH)]
        solved = jnp.concatenate(
            [dot_left(inverse * carry, key), dot_left(inverse, value)], axis=1
        )
        solved_ref[h, c] = solved.astype(BF16)
        moved = dot_right(key, scale * solved, TN)
        maps[c, h] = (
            jnp.where(eye, fade, 0.0) - moved[:, :DH],
            moved[:, DH:],
        )
    for h in range(heads):
        joined = jnp.concatenate(maps[0, h], axis=1)
        for c in range(1, chunks):
            before_ref[h, c - 1] = joined.astype(BF16)
            step_map, step_offset = maps[c, h]
            moved = dot_wide(step_map, joined)
            joined = jnp.concatenate([moved[:, :DH], moved[:, DH:] + step_offset], axis=1)
        result = joined.astype(BF16)

        @pl.when(core == h // 2)
        def _(result=result, h=h):
            mine_ref[h % 2] = result

        @pl.when(core != h // 2)
        def _(result=result, h=h):
            theirs_ref[h % 2] = result


def read_kernel(heads, chunks, q_ref, k_ref, solved_ref, before_ref, rows_ref, lead_ref, local_ref):
    keys_all = k_ref.reshape(2 * k_ref.shape[0], k_ref.shape[2])
    token, step = iotas(ROWS, STEPS)
    for h in range(heads):
        for c in range(chunks):
            query = q_ref[pl.ds(c * ROWS, ROWS), pl.ds(h * DH, DH)]
            key = keys_all[pl.ds(c * STEPS, STEPS), pl.ds(h * DH, DH)]
            lines = rows_ref[h, c]
            total, weight = lines[0:1], lines[1:2]
            at_token = jnp.sum(jnp.where(step == 2 * token, total, 0.0), axis=1, keepdims=True)
            visible = 2 * token + 1 >= step
            decay = jnp.exp(jnp.minimum(at_token - total, 0.0))
            scores = jnp.where(visible, dot(query, key, NT) * decay * weight, 0.0)
            seen = dot(scores.astype(BF16), solved_ref[h, c])
            lead = jnp.exp(at_token) * query.astype(F32) - seen[:, :DH]
            local = seen[:, DH:]
            if c:
                moved = dot(lead.astype(BF16), before_ref[h, c - 1])
                lead = moved[:, :DH]
                local = local + moved[:, DH:]
            lead_ref[h, pl.ds(c * ROWS, ROWS)] = lead.astype(BF16)
            local_ref[h, pl.ds(c * ROWS, ROWS)] = local


def pair_kernel(place_ref, mine_ref, other_ref, first_ref, pair_ref):
    core = place_ref[0]
    for h in range(2):
        mine, other = mine_ref[h].astype(F32), other_ref[h].astype(F32)
        first = jnp.where(core == 0, mine, other).astype(BF16)
        second = jnp.where(core == 0, other, mine)
        first_ref[h] = first
        moved = dot(second[:, :DH].astype(BF16), first)
        pair_ref[h] = jnp.concatenate(
            [moved[:, :DH], moved[:, DH:] + second[:, DH:]], axis=1
        ).astype(BF16)


def ring_kernel(place_ref, own_ref, one_ref, two_ref, three_ref, before_ref, whole_ref, offset_ref, slots):
    y = place_ref[1]
    for back, ref in enumerate((own_ref, one_ref, two_ref, three_ref)):
        slots[lax.rem(y - back + 4, 4)] = ref[...]
    row, column = iotas(DH, 2 * DH)
    nothing = (row == column).astype(F32)
    joined = [slots[0, h].astype(F32) for h in range(2)]
    before = [jnp.where(y == 1, joined[h], nothing) for h in range(2)]
    for k in range(1, 4):
        for h in range(2):
            step = slots[k, h]
            moved = dot_right(step[:, :DH], joined[h])
            joined[h] = jnp.concatenate(
                [moved[:, :DH], moved[:, DH:] + step[:, DH:].astype(F32)], axis=1
            )
            if k < 3:
                before[h] = jnp.where(y == k + 1, joined[h], before[h])
    for h in range(2):
        before_ref[h] = before[h]
        whole_ref[h] = joined[h].astype(BF16)
        offset_ref[h] = joined[h][:, DH:].astype(BF16)


def state_kernel(place_ref, first_ref, before_ref, one_ref, two_ref, three_ref, keep_ref, send_ref):
    core = place_ref[0]
    for h in range(2):
        state = three_ref[h].astype(F32)
        for ref in (two_ref, one_ref):
            state = dot_right(ref[h, :, :DH], state) + ref[h, :, DH:].astype(F32)
        chip = dot_wide(before_ref[h, :, :DH], state) + before_ref[h, :, DH:]
        later = dot_right(first_ref[h, :, :DH], chip) + first_ref[h, :, DH:].astype(F32)
        keep_ref[h] = jnp.where(core == 0, chip, later).astype(BF16)
        send_ref[h] = jnp.where(core == 0, later, chip).astype(BF16)


def output_kernel(heads, place_ref, lead_ref, local_ref, keep_ref, other_ref, gain_ref, weight_ref, out_ref, states):
    core = place_ref[0]
    states[pl.ds(core * 2, 2)] = keep_ref[...]
    states[pl.ds((1 - core) * 2, 2)] = other_ref[...]
    normed = []
    for h in range(heads):
        read = dot(lead_ref[h], states[h]) + local_ref[h]
        scale = lax.rsqrt(jnp.mean(read * read, axis=1, keepdims=True) + 1e-06)
        normed.append((read * scale * gain_ref[:, pl.ds(h * DH, DH)]).astype(BF16))
    flat = jnp.concatenate(normed, axis=1)
    width = 512
    for j in range(0, out_ref.shape[1], width):
        out_ref[:, pl.ds(j, width)] = dot(flat, weight_ref[:, pl.ds(j, width)]).astype(BF16)


def call(kernel, outs, args, scratch=(), flops=0):
    moved = sum(a.size * a.dtype.itemsize for a in (*args, *outs))
    specs = [SMEM if a.dtype == jnp.int32 else VMEM for a in args]
    return pl.pallas_call(
        kernel,
        out_shape=tuple(outs),
        in_specs=specs,
        out_specs=tuple(VMEM for _ in outs),
        scratch_shapes=list(scratch),
        compiler_params=pltpu.CompilerParams(vmem_limit_bytes=40 * 2**20),
        cost_estimate=pl.CostEstimate(flops=flops, bytes_accessed=moved, transcendentals=0),
    )(*args)


def on_device(queries, keys, values, beta, log_gate, norm_gain, out_weight):
    heads = beta.shape[0]
    tokens = queries.shape[0]
    chunks = tokens // ROWS
    shape = jax.ShapeDtypeStruct
    ctx = lax.axis_index("ctx")
    place = jnp.stack([ctx % 2, (ctx // 2) % 4, ctx // 8]).astype(jnp.int32)
    devices = range(32)

    def y_shift(block, d):
        route = [(i, (i // 8) * 8 + ((i // 2 + d) % 4) * 2 + i % 2) for i in devices]
        return lax.ppermute(block, "ctx", route)

    def x_shift(block, d):
        return lax.ppermute(block, "ctx", [(i, i + 8 * d) for i in devices if i + 8 * d < 32])

    def swap(block):
        return lax.ppermute(block, "ctx", [(i, i ^ 1) for i in devices])

    pair_shape = shape((2, DH, 2 * DH), BF16)
    mine, theirs, solved, before, rows = call(
        functools.partial(local_kernel, heads, chunks),
        [
            pair_shape,
            pair_shape,
            shape((heads, chunks, STEPS, 2 * DH), BF16),
            shape((heads, chunks - 1, DH, 2 * DH), BF16),
            shape((heads, chunks, 8, STEPS), F32),
        ],
        [place, keys, values, beta, log_gate],
        flops=50 * heads * chunks * 2 * DH**3,
    )
    other = swap(theirs)
    lead, local = call(
        functools.partial(read_kernel, heads, chunks),
        [shape((heads, tokens, DH), BF16), shape((heads, tokens, DH), F32)],
        [queries, keys, solved, before, rows],
        flops=3 * heads * chunks * 2 * DH**3,
    )
    first, pair = call(pair_kernel, [pair_shape, pair_shape], [place, mine, other])
    ring = [y_shift(pair, d) for d in (1, 2, 3)]
    chip_before, whole, offset = call(
        ring_kernel,
        [shape((2, DH, 2 * DH), F32), pair_shape, shape((2, DH, DH), BF16)],
        [place, pair, *ring],
        scratch=[pltpu.VMEM((4, 2, DH, 2 * DH), BF16)],
    )
    shifts = [x_shift(whole, 1), x_shift(whole, 2), x_shift(offset, 3)]
    keep, send = call(
        state_kernel,
        [shape((2, DH, DH), BF16)] * 2,
        [place, first, chip_before, *shifts],
    )
    received = swap(send)
    (partial,) = call(
        functools.partial(output_kernel, heads),
        [shape((tokens, out_weight.shape[1]), BF16)],
        [place, lead, local, keep, received, norm_gain.reshape(1, -1), out_weight],
        scratch=[pltpu.VMEM((heads, DH, DH), BF16)],
        flops=2 * tokens * out_weight.size,
    )
    return lax.psum_scatter(partial, "head", scatter_dimension=0, tiled=True)


def solution(mesh):
    return jax.shard_map(
        on_device,
        mesh=mesh,
        in_specs=(
            P("ctx", "head"),
            P("ctx", None, "head"),
            P("ctx", None, "head"),
            P("head", None, "ctx"),
            P("head", "ctx"),
            P("head"),
            P("head", None),
        ),
        out_specs=P(("ctx", "head"), None),
        check_vma=False,
    )
```

```python
import functools

import jax
import jax.numpy as jnp
from jax import lax
from jax.experimental import pallas as pl
from jax.experimental.pallas import tpu as pltpu
from jax.sharding import PartitionSpec as P

DH = 128
STEPS = 128
ROWS = STEPS // 2
F32 = jnp.float32
BF16 = jnp.bfloat16
NN = (((1,), (0,)), ((), ()))
NT = (((1,), (1,)), ((), ()))
TN = (((0,), (0,)), ((), ()))
VMEM = pl.BlockSpec(memory_space=pltpu.VMEM)
SMEM = pl.BlockSpec(memory_space=pltpu.SMEM)


def dot(a, b, dims=NN):
    return lax.dot_general(a, b, dims, preferred_element_type=F32)


def split(x):
    high = x.astype(BF16)
    return high, (x - high.astype(F32)).astype(BF16)


def dot_wide(a, b, dims=NN):
    a_high, a_low = split(a)
    b_high, b_low = split(b)
    return dot(a_high, b_high, dims) + (dot(a_high, b_low, dims) + dot(a_low, b_high, dims))


def dot_left(a, b, dims=NN):
    high, low = split(a)
    return dot(high, b, dims) + dot(low, b, dims)


def dot_right(a, b, dims=NN):
    high, low = split(b)
    return dot(a, high, dims) + dot(a, low, dims)


def iotas(rows, columns):
    return (
        lax.broadcasted_iota(jnp.int32, (rows, columns), 0),
        lax.broadcasted_iota(jnp.int32, (rows, columns), 1),
    )


def gate_sums(gates, betas):
    token, step = iotas(ROWS, STEPS)
    high = lax.Precision.HIGHEST
    upto = (2 * token <= step).astype(F32)
    sums = jnp.dot(gates, upto, precision=high, preferred_element_type=F32)
    even = (2 * token == step).astype(F32)
    odd = (2 * token + 1 == step).astype(F32)
    spread = jnp.dot(betas[0], even, precision=high, preferred_element_type=F32) + jnp.dot(
        betas[1], odd, precision=high, preferred_element_type=F32
    )
    return sums, spread


def unit_inverses(lowers):
    row, column = iotas(STEPS, STEPS)
    eye = (row == column).astype(F32)
    pairs = (row // 2 == column // 2) & (row > column)
    inverses = [eye - jnp.where(pairs, lower, 0.0) for lower in lowers]
    size = 2
    while size < STEPS:
        corner = (row // (2 * size) == column // (2 * size)) & (row // size > column // size)
        corners = [jnp.where(corner, lower, 0.0) for lower in lowers]
        parts = [split(inverse) for inverse in inverses]
        rights = [
            dot_right_parts(split(block), part) for block, part in zip(corners, parts)
        ]
        inverses = [
            inverse - dot_right_parts(part, split(right))
            for inverse, part, right in zip(inverses, parts, rights)
        ]
        size *= 2
    return inverses


def dot_right_parts(a, b):
    high, low = b
    top = jnp.concatenate([high, low], axis=1)
    bottom = jnp.concatenate([high, jnp.zeros_like(low)], axis=1)
    both = dot(jnp.concatenate(a, axis=1), jnp.concatenate([top, bottom], axis=0))
    return both[:, :STEPS] + both[:, STEPS:]


def local_kernel(
    heads, chunks, place_ref, k_hbm, v_hbm, beta_hbm, gate_hbm,
    mine_ref, theirs_ref, solved_ref, before_ref, rows_ref,
    k_ref, v_ref, beta_ref, gate_ref, arrived,
):
    core = place_ref[0]
    pairs = ((gate_hbm, gate_ref), (beta_hbm, beta_ref), (k_hbm, k_ref), (v_hbm, v_ref))
    copies = [pltpu.make_async_copy(a, b, arrived.at[i]) for i, (a, b) in enumerate(pairs)]
    for copy in copies:
        copy.start()
    for copy in copies[:3]:
        copy.wait()
    keys_all = k_ref.reshape(2 * k_ref.shape[0], k_ref.shape[2])
    values_all = v_ref.reshape(2 * v_ref.shape[0], v_ref.shape[2])
    row, column = iotas(STEPS, STEPS)
    eye = row == column
    strict = row > column

    def down(line):
        return jnp.sum(jnp.where(eye, line, 0.0), axis=1, keepdims=True)

    def across(stack):
        return jnp.sum(jnp.where(eye, stack, 0.0), axis=0, keepdims=True)

    work = []
    for c in range(chunks):
        at = pl.ds(c * ROWS, ROWS)
        gates = jnp.maximum(gate_ref[:, at], -200.0)
        sums, spread = gate_sums(gates, (beta_ref[:, 0, at], beta_ref[:, 1, at]))
        for h in range(heads):
            key = keys_all[pl.ds(c * STEPS, STEPS), pl.ds(h * DH, DH)]
            wide = key.astype(F32)
            norm = lax.rsqrt(jnp.sum(wide * wide, axis=1, keepdims=True) + 1e-06)
            norm_line = across(norm)
            total = sums[h : h + 1]
            total_down = down(total)
            beta_line = spread[h : h + 1]
            inner = dot(key, key, NT)
            decay = jnp.exp(jnp.minimum(total_down - total, 0.0))
            lower = jnp.where(strict, decay * (inner * norm) * (norm_line * beta_line), 0.0)
            rows_ref[h, c] = jnp.concatenate(
                [total, beta_line * norm_line, jnp.zeros((6, STEPS), F32)], axis=0
            )
            last = total[:, STEPS - 1 :]
            scale = jnp.exp(jnp.minimum(last - total_down, 0.0)) * down(beta_line) * norm
            work.append((c, h, key, lower, jnp.exp(total) * norm_line, scale, jnp.exp(last)))
    inverses = unit_inverses([w[3] for w in work])
    maps = {}
    copies[3].wait()
    for (c, h, key, _, carry, scale, fade), inverse in zip(work, inverses):
        value = values_all[pl.ds(c * STEPS, STEPS), pl.ds(h * DH, DH)]
        solved = jnp.concatenate(
            [dot_left(inverse * carry, key), dot_left(inverse, value)], axis=1
        )
        solved_ref[h, c] = solved.astype(BF16)
        moved = dot_right(key, scale * solved, TN)
        maps[c, h] = (
            jnp.where(eye, fade, 0.0) - moved[:, :DH],
            moved[:, DH:],
        )
    for h in range(heads):
        joined = jnp.concatenate(maps[0, h], axis=1)
        for c in range(1, chunks):
            before_ref[h, c - 1] = joined.astype(BF16)
            step_map, step_offset = maps[c, h]
            moved = dot_wide(step_map, joined)
            joined = jnp.concatenate([moved[:, :DH], moved[:, DH:] + step_offset], axis=1)
        result = joined.astype(BF16)

        @pl.when(core == h // 2)
        def _(result=result, h=h):
            mine_ref[h % 2] = result

        @pl.when(core != h // 2)
        def _(result=result, h=h):
            theirs_ref[h % 2] = result


def read_kernel(heads, chunks, q_ref, k_ref, solved_ref, before_ref, rows_ref, lead_ref, local_ref):
    keys_all = k_ref.reshape(2 * k_ref.shape[0], k_ref.shape[2])
    token, step = iotas(ROWS, STEPS)
    for h in range(heads):
        for c in range(chunks):
            query = q_ref[pl.ds(c * ROWS, ROWS), pl.ds(h * DH, DH)]
            key = keys_all[pl.ds(c * STEPS, STEPS), pl.ds(h * DH, DH)]
            lines = rows_ref[h, c]
            total, weight = lines[0:1], lines[1:2]
            at_token = jnp.sum(jnp.where(step == 2 * token, total, 0.0), axis=1, keepdims=True)
            visible = 2 * token + 1 >= step
            decay = jnp.exp(jnp.minimum(at_token - total, 0.0))
            scores = jnp.where(visible, dot(query, key, NT) * decay * weight, 0.0)
            seen = dot(scores.astype(BF16), solved_ref[h, c])
            lead = jnp.exp(at_token) * query.astype(F32) - seen[:, :DH]
            local = seen[:, DH:]
            if c:
                moved = dot(lead.astype(BF16), before_ref[h, c - 1])
                lead = moved[:, :DH]
                local = local + moved[:, DH:]
            lead_ref[h, pl.ds(c * ROWS, ROWS)] = lead.astype(BF16)
            local_ref[h, pl.ds(c * ROWS, ROWS)] = local


def pair_kernel(place_ref, mine_ref, other_ref, first_ref, pair_ref):
    core = place_ref[0]
    for h in range(2):
        mine, other = mine_ref[h].astype(F32), other_ref[h].astype(F32)
        first = jnp.where(core == 0, mine, other).astype(BF16)
        second = jnp.where(core == 0, other, mine)
        first_ref[h] = first
        moved = dot(second[:, :DH].astype(BF16), first)
        pair_ref[h] = jnp.concatenate(
            [moved[:, :DH], moved[:, DH:] + second[:, DH:]], axis=1
        ).astype(BF16)


def ring_kernel(place_ref, own_ref, one_ref, two_ref, three_ref, before_ref, whole_ref, offset_ref, slots):
    y = place_ref[1]
    for back, ref in enumerate((own_ref, one_ref, two_ref, three_ref)):
        slots[lax.rem(y - back + 4, 4)] = ref[...]
    row, column = iotas(DH, 2 * DH)
    nothing = (row == column).astype(F32)
    joined = [slots[0, h].astype(F32) for h in range(2)]
    before = [jnp.where(y == 1, joined[h], nothing) for h in range(2)]
    for k in range(1, 4):
        for h in range(2):
            step = slots[k, h]
            moved = dot_right(step[:, :DH], joined[h])
            joined[h] = jnp.concatenate(
                [moved[:, :DH], moved[:, DH:] + step[:, DH:].astype(F32)], axis=1
            )
            if k < 3:
                before[h] = jnp.where(y == k + 1, joined[h], before[h])
    for h in range(2):
        before_ref[h] = before[h]
        whole_ref[h] = joined[h].astype(BF16)
        offset_ref[h] = joined[h][:, DH:].astype(BF16)


def state_kernel(place_ref, first_ref, before_ref, one_ref, two_ref, three_ref, keep_ref, send_ref):
    core = place_ref[0]
    for h in range(2):
        state = three_ref[h].astype(F32)
        for ref in (two_ref, one_ref):
            state = dot_right(ref[h, :, :DH], state) + ref[h, :, DH:].astype(F32)
        chip = dot_wide(before_ref[h, :, :DH], state) + before_ref[h, :, DH:]
        later = dot_right(first_ref[h, :, :DH], chip) + first_ref[h, :, DH:].astype(F32)
        keep_ref[h] = jnp.where(core == 0, chip, later).astype(BF16)
        send_ref[h] = jnp.where(core == 0, later, chip).astype(BF16)


def normed_kernel(
    heads, place_ref, lead_ref, local_ref, keep_ref, other_ref, gain_ref,
    own_ref, back_ref, ahead_ref, states, normed,
):
    core, z = place_ref[0], place_ref[3]
    way = 1 - 2 * core
    states[pl.ds(core * 2, 2)] = keep_ref[...]
    states[pl.ds((1 - core) * 2, 2)] = other_ref[...]
    for h in range(heads):
        read = dot(lead_ref[h], states[h]) + local_ref[h]
        scale = lax.rsqrt(jnp.mean(read * read, axis=1, keepdims=True) + 1e-06)
        lanes = pl.ds(h * DH, DH)
        normed[:, lanes] = (read * scale * gain_ref[:, lanes]).astype(BF16)
    block = own_ref.shape[0] // 3
    for ref, offsets in ((own_ref, (0, 3, -2)), (back_ref, (-1, 2, -3)), (ahead_ref, (1, 4))):
        for i, offset in enumerate(offsets):
            at = lax.rem(z + way * offset + 8, 8) * block
            ref[pl.ds(i * block, block)] = normed[pl.ds(pl.multiple_of(at, block), block)]


def columns(ref, width=512):
    return [pl.ds(j, width) for j in range(0, ref.shape[1], width)]


def own_kernel(rows_ref, weight_ref, sum_ref):
    rows = rows_ref[...]
    for at in columns(sum_ref):
        sum_ref[:, at] = dot(rows, weight_ref[:, at])


def next_kernel(rows_ref, weight_ref, sum_ref, two_ref, rest_ref):
    rows = rows_ref[...]
    kept = rest_ref.shape[0]
    for at in columns(sum_ref):
        total = sum_ref[:, at] + dot(rows, weight_ref[:, at])
        rest_ref[:, at] = total[:kept]
        two_ref[:, at] = total[kept:].astype(BF16)


def last_kernel(rows_ref, weight_ref, sum_ref, keep_ref, three_ref):
    rows = rows_ref[...]
    kept = keep_ref.shape[0]
    for at in columns(sum_ref):
        total = sum_ref[:, at] + dot(rows, weight_ref[:, at])
        keep_ref[:, at] = total[:kept]
        three_ref[:, at] = total[kept:].astype(BF16)


def add_kernel(keep_ref, two_ref, three_ref, out_ref):
    out_ref[...] = (keep_ref[...] + (two_ref[...].astype(F32) + three_ref[...].astype(F32))).astype(BF16)


def call(kernel, outs, args, scratch=(), flops=0, limit=16, space=pltpu.VMEM):
    moved = sum(a.size * a.dtype.itemsize for a in (*args, *outs))
    specs = [SMEM if a.dtype == jnp.int32 else pl.BlockSpec(memory_space=space) for a in args]
    return pl.pallas_call(
        kernel,
        out_shape=tuple(outs),
        in_specs=specs,
        out_specs=tuple(VMEM for _ in outs),
        scratch_shapes=list(scratch),
        compiler_params=pltpu.CompilerParams(vmem_limit_bytes=limit * 2**20),
        cost_estimate=pl.CostEstimate(flops=flops, bytes_accessed=moved, transcendentals=0),
    )(*args)


def on_device(queries, keys, values, beta, log_gate, norm_gain, out_weight):
    heads = beta.shape[0]
    tokens = queries.shape[0]
    chunks = tokens // ROWS
    shape = jax.ShapeDtypeStruct
    ctx = lax.axis_index("ctx")
    head = lax.axis_index("head")
    place = jnp.stack([ctx % 2, (ctx // 2) % 4, ctx // 8, head]).astype(jnp.int32)
    devices = range(32)

    def y_shift(block, d):
        route = [(i, (i // 8) * 8 + ((i // 2 + d) % 4) * 2 + i % 2) for i in devices]
        return lax.ppermute(block, "ctx", route)

    def x_shift(block, d):
        return lax.ppermute(block, "ctx", [(i, i + 8 * d) for i in devices if i + 8 * d < 32])

    def swap(block):
        return lax.ppermute(block, "ctx", [(i, i ^ 1) for i in devices])

    def z_shift(block, d):
        route = [
            (i * 8 + z, i * 8 + (z + (d if i % 2 == 0 else -d)) % 8) for i in devices for z in range(8)
        ]
        return lax.ppermute(block, ("ctx", "head"), route)

    next_weight = z_shift(out_weight, -1)
    pair_shape = shape((2, DH, 2 * DH), BF16)
    mine, theirs, solved, before, rows = call(
        functools.partial(local_kernel, heads, chunks),
        [
            pair_shape,
            pair_shape,
            shape((heads, chunks, STEPS, 2 * DH), BF16),
            shape((heads, chunks - 1, DH, 2 * DH), BF16),
            shape((heads, chunks, 8, STEPS), F32),
        ],
        [place, *(pltpu.with_memory_space_constraint(a, pltpu.HBM) for a in (keys, values, beta, log_gate))],
        scratch=[pltpu.VMEM(a.shape, a.dtype) for a in (keys, values, beta, log_gate)]
        + [pltpu.SemaphoreType.DMA((4,))],
        flops=50 * heads * chunks * 2 * DH**3,
        space=pltpu.HBM,
    )
    other = swap(theirs)
    lead, local = call(
        functools.partial(read_kernel, heads, chunks),
        [shape((heads, tokens, DH), BF16), shape((heads, tokens, DH), F32)],
        [queries, keys, solved, before, rows],
        flops=3 * heads * chunks * 2 * DH**3,
    )
    first, pair = call(pair_kernel, [pair_shape, pair_shape], [place, mine, other])
    ring = [y_shift(pair, d) for d in (1, 2, 3)]
    *ring, lead, local = lax.optimization_barrier((*ring, lead, local))
    chip_before, whole, offset = call(
        ring_kernel,
        [shape((2, DH, 2 * DH), F32), pair_shape, shape((2, DH, DH), BF16)],
        [place, pair, *ring],
        scratch=[pltpu.VMEM((4, 2, DH, 2 * DH), BF16)],
    )
    shifts = [x_shift(whole, 1), x_shift(whole, 2), x_shift(offset, 3)]
    keep, send = call(
        state_kernel,
        [shape((2, DH, DH), BF16)] * 2,
        [place, first, chip_before, *shifts],
    )
    received = swap(send)
    block = tokens // 8
    width = heads * DH
    own, back, ahead = call(
        functools.partial(normed_kernel, heads),
        [shape((3 * block, width), BF16), shape((3 * block, width), BF16), shape((2 * block, width), BF16)],
        [place, lead, local, keep, received, norm_gain.reshape(1, -1)],
        scratch=[pltpu.VMEM((heads, DH, DH), BF16), pltpu.VMEM((tokens, width), BF16)],
        flops=2 * tokens * width * DH,
    )
    next_rows = z_shift(back, -1)
    last_rows = z_shift(ahead, 1)
    out_width = out_weight.shape[1]
    (total,) = call(
        own_kernel,
        [shape((3 * block, out_width), F32)],
        [own, out_weight],
        flops=2 * own.shape[0] * out_weight.size,
        limit=24,
    )
    next_weight, next_rows, total = lax.optimization_barrier((next_weight, next_rows, total))
    last_weight = swap(next_weight)
    two, total = call(
        next_kernel,
        [shape((block, out_width), BF16), shape((2 * block, out_width), F32)],
        [next_rows, next_weight, total],
        flops=2 * next_rows.shape[0] * out_weight.size,
        limit=24,
    )
    two = z_shift(two, -2)
    kept, three = call(
        last_kernel,
        [shape((block, out_width), F32), shape((block, out_width), BF16)],
        [last_rows, last_weight, total],
        flops=2 * last_rows.shape[0] * out_weight.size,
        limit=24,
    )
    three = z_shift(three, 3)
    (out,) = call(add_kernel, [shape((block, out_width), BF16)], [kept, two, three])
    return out


def solution(mesh):
    return jax.shard_map(
        on_device,
        mesh=mesh,
        in_specs=(
            P("ctx", "head"),
            P("ctx", None, "head"),
            P("ctx", None, "head"),
            P("head", None, "ctx"),
            P("head", "ctx"),
            P("head"),
            P("head", None),
        ),
        out_specs=P(("ctx", "head"), None),
        check_vma=False,
    )
```

```python
import functools

import jax
import jax.numpy as jnp
from jax import lax
from jax.experimental import pallas as pl
from jax.experimental.pallas import tpu as pltpu
from jax.sharding import PartitionSpec as P

DH = 128
STEPS = 128
ROWS = STEPS // 2
F32 = jnp.float32
BF16 = jnp.bfloat16
NN = (((1,), (0,)), ((), ()))
NT = (((1,), (1,)), ((), ()))
TN = (((0,), (0,)), ((), ()))
VMEM = pl.BlockSpec(memory_space=pltpu.VMEM)
SMEM = pl.BlockSpec(memory_space=pltpu.SMEM)


def dot(a, b, dims=NN):
    return lax.dot_general(a, b, dims, preferred_element_type=F32)


def split(x):
    high = x.astype(BF16)
    return high, (x - high.astype(F32)).astype(BF16)


def dot_wide(a, b, dims=NN):
    a_high, a_low = split(a)
    b_high, b_low = split(b)
    return dot(a_high, b_high, dims) + (dot(a_high, b_low, dims) + dot(a_low, b_high, dims))


def dot_left(a, b, dims=NN):
    high, low = split(a)
    return dot(high, b, dims) + dot(low, b, dims)


def dot_right(a, b, dims=NN):
    high, low = split(b)
    return dot(a, high, dims) + dot(a, low, dims)


def iotas(rows, columns):
    return (
        lax.broadcasted_iota(jnp.int32, (rows, columns), 0),
        lax.broadcasted_iota(jnp.int32, (rows, columns), 1),
    )


def gate_sums(gates, betas):
    token, step = iotas(ROWS, STEPS)
    high = lax.Precision.HIGHEST
    upto = (2 * token <= step).astype(F32)
    sums = jnp.dot(gates, upto, precision=high, preferred_element_type=F32)
    even = (2 * token == step).astype(F32)
    odd = (2 * token + 1 == step).astype(F32)
    spread = jnp.dot(betas[0], even, precision=high, preferred_element_type=F32) + jnp.dot(
        betas[1], odd, precision=high, preferred_element_type=F32
    )
    return sums, spread


def unit_inverses(lowers):
    row, column = iotas(STEPS, STEPS)
    eye = (row == column).astype(F32)
    pairs = (row // 2 == column // 2) & (row > column)
    inverses = [eye - jnp.where(pairs, lower, 0.0) for lower in lowers]
    size = 2
    while size < STEPS:
        corner = (row // (2 * size) == column // (2 * size)) & (row // size > column // size)
        corners = [jnp.where(corner, lower, 0.0) for lower in lowers]
        parts = [split(inverse) for inverse in inverses]
        rights = [
            dot_right_parts(split(block), part) for block, part in zip(corners, parts)
        ]
        inverses = [
            inverse - dot_right_parts(part, split(right))
            for inverse, part, right in zip(inverses, parts, rights)
        ]
        size *= 2
    return inverses


def dot_right_parts(a, b):
    high, low = b
    top = jnp.concatenate([high, low], axis=1)
    bottom = jnp.concatenate([high, jnp.zeros_like(low)], axis=1)
    both = dot(jnp.concatenate(a, axis=1), jnp.concatenate([top, bottom], axis=0))
    return both[:, :STEPS] + both[:, STEPS:]


def local_kernel(
    heads, chunks, place_ref, k_hbm, v_hbm, beta_hbm, gate_hbm,
    mine_ref, theirs_ref, solved_ref, before_ref, rows_ref,
    k_ref, v_ref, beta_ref, gate_ref, arrived,
):
    core = place_ref[0]
    pairs = ((gate_hbm, gate_ref), (beta_hbm, beta_ref), (k_hbm, k_ref), (v_hbm, v_ref))
    copies = [pltpu.make_async_copy(a, b, arrived.at[i]) for i, (a, b) in enumerate(pairs)]
    for copy in copies:
        copy.start()
    for copy in copies[:3]:
        copy.wait()
    keys_all = k_ref.reshape(2 * k_ref.shape[0], k_ref.shape[2])
    values_all = v_ref.reshape(2 * v_ref.shape[0], v_ref.shape[2])
    row, column = iotas(STEPS, STEPS)
    eye = row == column
    strict = row > column

    def down(line):
        return jnp.sum(jnp.where(eye, line, 0.0), axis=1, keepdims=True)

    def across(stack):
        return jnp.sum(jnp.where(eye, stack, 0.0), axis=0, keepdims=True)

    work = []
    for c in range(chunks):
        at = pl.ds(c * ROWS, ROWS)
        gates = jnp.maximum(gate_ref[:, at], -200.0)
        sums, spread = gate_sums(gates, (beta_ref[:, 0, at], beta_ref[:, 1, at]))
        for h in range(heads):
            key = keys_all[pl.ds(c * STEPS, STEPS), pl.ds(h * DH, DH)]
            wide = key.astype(F32)
            norm = lax.rsqrt(jnp.sum(wide * wide, axis=1, keepdims=True) + 1e-06)
            norm_line = across(norm)
            total = sums[h : h + 1]
            total_down = down(total)
            beta_line = spread[h : h + 1]
            inner = dot(key, key, NT)
            decay = jnp.exp(jnp.minimum(total_down - total, 0.0))
            lower = jnp.where(strict, decay * (inner * norm) * (norm_line * beta_line), 0.0)
            rows_ref[h, c] = jnp.concatenate(
                [total, beta_line * norm_line, jnp.zeros((6, STEPS), F32)], axis=0
            )
            last = total[:, STEPS - 1 :]
            scale = jnp.exp(jnp.minimum(last - total_down, 0.0)) * down(beta_line) * norm
            work.append((c, h, key, lower, jnp.exp(total) * norm_line, scale, jnp.exp(last)))
    inverses = unit_inverses([w[3] for w in work])
    maps = {}
    copies[3].wait()
    for (c, h, key, _, carry, scale, fade), inverse in zip(work, inverses):
        value = values_all[pl.ds(c * STEPS, STEPS), pl.ds(h * DH, DH)]
        solved = jnp.concatenate(
            [dot_left(inverse * carry, key), dot_left(inverse, value)], axis=1
        )
        solved_ref[h, c] = solved.astype(BF16)
        moved = dot_right(key, scale * solved, TN)
        maps[c, h] = (
            jnp.where(eye, fade, 0.0) - moved[:, :DH],
            moved[:, DH:],
        )
    for h in range(heads):
        joined = jnp.concatenate(maps[0, h], axis=1)
        for c in range(1, chunks):
            before_ref[h, c - 1] = joined.astype(BF16)
            step_map, step_offset = maps[c, h]
            moved = dot_wide(step_map, joined)
            joined = jnp.concatenate([moved[:, :DH], moved[:, DH:] + step_offset], axis=1)
        result = joined.astype(BF16)

        @pl.when(core == h // 2)
        def _(result=result, h=h):
            mine_ref[h % 2] = result

        @pl.when(core != h // 2)
        def _(result=result, h=h):
            theirs_ref[h % 2] = result


def read_kernel(heads, chunks, q_ref, k_ref, solved_ref, before_ref, rows_ref, lead_ref, local_ref):
    keys_all = k_ref.reshape(2 * k_ref.shape[0], k_ref.shape[2])
    token, step = iotas(ROWS, STEPS)
    for h in range(heads):
        for c in range(chunks):
            query = q_ref[pl.ds(c * ROWS, ROWS), pl.ds(h * DH, DH)]
            key = keys_all[pl.ds(c * STEPS, STEPS), pl.ds(h * DH, DH)]
            lines = rows_ref[h, c]
            total, weight = lines[0:1], lines[1:2]
            at_token = jnp.sum(jnp.where(step == 2 * token, total, 0.0), axis=1, keepdims=True)
            visible = 2 * token + 1 >= step
            decay = jnp.exp(jnp.minimum(at_token - total, 0.0))
            scores = jnp.where(visible, dot(query, key, NT) * decay * weight, 0.0)
            seen = dot(scores.astype(BF16), solved_ref[h, c])
            lead = jnp.exp(at_token) * query.astype(F32) - seen[:, :DH]
            local = seen[:, DH:]
            if c:
                moved = dot(lead.astype(BF16), before_ref[h, c - 1])
                lead = moved[:, :DH]
                local = local + moved[:, DH:]
            lead_ref[h, pl.ds(c * ROWS, ROWS)] = lead.astype(BF16)
            local_ref[h, pl.ds(c * ROWS, ROWS)] = local


def pair_kernel(place_ref, mine_ref, other_ref, first_ref, pair_ref):
    core = place_ref[0]
    for h in range(2):
        mine, other = mine_ref[h].astype(F32), other_ref[h].astype(F32)
        first = jnp.where(core == 0, mine, other).astype(BF16)
        second = jnp.where(core == 0, other, mine)
        first_ref[h] = first
        moved = dot(second[:, :DH].astype(BF16), first)
        pair_ref[h] = jnp.concatenate(
            [moved[:, :DH], moved[:, DH:] + second[:, DH:]], axis=1
        ).astype(BF16)


def ring_kernel(place_ref, own_ref, one_ref, two_ref, three_ref, before_ref, whole_ref, offset_ref, slots):
    y = place_ref[1]
    for back, ref in enumerate((own_ref, one_ref, two_ref, three_ref)):
        slots[lax.rem(y - back + 4, 4)] = ref[...]
    row, column = iotas(DH, 2 * DH)
    nothing = (row == column).astype(F32)
    joined = [slots[0, h].astype(F32) for h in range(2)]
    before = [jnp.where(y == 1, joined[h], nothing) for h in range(2)]
    for k in range(1, 4):
        for h in range(2):
            step = slots[k, h]
            moved = dot_right(step[:, :DH], joined[h])
            joined[h] = jnp.concatenate(
                [moved[:, :DH], moved[:, DH:] + step[:, DH:].astype(F32)], axis=1
            )
            if k < 3:
                before[h] = jnp.where(y == k + 1, joined[h], before[h])
    for h in range(2):
        before_ref[h] = before[h]
        whole_ref[h] = joined[h].astype(BF16)
        offset_ref[h] = joined[h][:, DH:].astype(BF16)


def state_kernel(place_ref, first_ref, before_ref, one_ref, two_ref, three_ref, keep_ref, send_ref):
    core = place_ref[0]
    for h in range(2):
        state = three_ref[h].astype(F32)
        for ref in (two_ref, one_ref):
            state = dot_right(ref[h, :, :DH], state) + ref[h, :, DH:].astype(F32)
        chip = dot_wide(before_ref[h, :, :DH], state) + before_ref[h, :, DH:]
        later = dot_right(first_ref[h, :, :DH], chip) + first_ref[h, :, DH:].astype(F32)
        keep_ref[h] = jnp.where(core == 0, chip, later).astype(BF16)
        send_ref[h] = jnp.where(core == 0, later, chip).astype(BF16)


def normed_kernel(
    heads, place_ref, lead_ref, local_ref, keep_ref, other_ref, gain_ref,
    own_ref, back_ref, ahead_ref, states, normed,
):
    core, z = place_ref[0], place_ref[3]
    way = 1 - 2 * core
    states[pl.ds(core * 2, 2)] = keep_ref[...]
    states[pl.ds((1 - core) * 2, 2)] = other_ref[...]
    for h in range(heads):
        read = dot(lead_ref[h], states[h]) + local_ref[h]
        scale = lax.rsqrt(jnp.mean(read * read, axis=1, keepdims=True) + 1e-06)
        lanes = pl.ds(h * DH, DH)
        normed[:, lanes] = (read * scale * gain_ref[:, lanes]).astype(BF16)
    block = own_ref.shape[0] // 3
    for ref, offsets in ((own_ref, (0, 3, -2)), (back_ref, (-1, 2, -3)), (ahead_ref, (1, 4))):
        for i, offset in enumerate(offsets):
            at = lax.rem(z + way * offset + 8, 8) * block
            ref[pl.ds(i * block, block)] = normed[pl.ds(pl.multiple_of(at, block), block)]


def columns(ref, width=512):
    return [pl.ds(j, width) for j in range(0, ref.shape[1], width)]


def own_kernel(rows_ref, weight_ref, sum_ref):
    rows = rows_ref[...]
    for at in columns(sum_ref):
        sum_ref[:, at] = dot(rows, weight_ref[:, at])


def next_kernel(next_ref, other_ref, weight_ref, sum_ref, two_ref, rest_ref, other_sum_ref):
    next_rows, other_rows = next_ref[...], other_ref[...]
    kept = rest_ref.shape[0]
    for at in columns(sum_ref):
        weights = weight_ref[:, at]
        total = sum_ref[:, at] + dot(next_rows, weights)
        rest_ref[:, at] = total[:kept]
        two_ref[:, at] = total[kept:].astype(BF16)
        other_sum_ref[:, at] = dot(other_rows, weights).astype(BF16)


def join_kernel(sum_ref, last_ref, keep_ref, three_ref):
    total = sum_ref[...] + last_ref[...].astype(F32)
    kept = keep_ref.shape[0]
    keep_ref[...] = total[:kept]
    three_ref[...] = total[kept:].astype(BF16)


def add_kernel(keep_ref, two_ref, three_ref, out_ref):
    out_ref[...] = (keep_ref[...] + (two_ref[...].astype(F32) + three_ref[...].astype(F32))).astype(BF16)


def call(kernel, outs, args, scratch=(), flops=0, limit=16, space=pltpu.VMEM):
    moved = sum(a.size * a.dtype.itemsize for a in (*args, *outs))
    specs = [SMEM if a.dtype == jnp.int32 else pl.BlockSpec(memory_space=space) for a in args]
    return pl.pallas_call(
        kernel,
        out_shape=tuple(outs),
        in_specs=specs,
        out_specs=tuple(VMEM for _ in outs),
        scratch_shapes=list(scratch),
        compiler_params=pltpu.CompilerParams(vmem_limit_bytes=limit * 2**20),
        cost_estimate=pl.CostEstimate(flops=flops, bytes_accessed=moved, transcendentals=0),
    )(*args)


def on_device(queries, keys, values, beta, log_gate, norm_gain, out_weight):
    heads = beta.shape[0]
    tokens = queries.shape[0]
    chunks = tokens // ROWS
    shape = jax.ShapeDtypeStruct
    ctx = lax.axis_index("ctx")
    head = lax.axis_index("head")
    place = jnp.stack([ctx % 2, (ctx // 2) % 4, ctx // 8, head]).astype(jnp.int32)
    devices = range(32)

    def y_shift(block, d):
        route = [(i, (i // 8) * 8 + ((i // 2 + d) % 4) * 2 + i % 2) for i in devices]
        return lax.ppermute(block, "ctx", route)

    def x_shift(block, d):
        return lax.ppermute(block, "ctx", [(i, i + 8 * d) for i in devices if i + 8 * d < 32])

    def swap(block):
        return lax.ppermute(block, "ctx", [(i, i ^ 1) for i in devices])

    def z_shift(block, d):
        route = [
            (i * 8 + z, i * 8 + (z + (d if i % 2 == 0 else -d)) % 8) for i in devices for z in range(8)
        ]
        return lax.ppermute(block, ("ctx", "head"), route)

    next_weight = z_shift(out_weight, -1)
    pair_shape = shape((2, DH, 2 * DH), BF16)
    mine, theirs, solved, before, rows = call(
        functools.partial(local_kernel, heads, chunks),
        [
            pair_shape,
            pair_shape,
            shape((heads, chunks, STEPS, 2 * DH), BF16),
            shape((heads, chunks - 1, DH, 2 * DH), BF16),
            shape((heads, chunks, 8, STEPS), F32),
        ],
        [place, *(pltpu.with_memory_space_constraint(a, pltpu.HBM) for a in (keys, values, beta, log_gate))],
        scratch=[pltpu.VMEM(a.shape, a.dtype) for a in (keys, values, beta, log_gate)]
        + [pltpu.SemaphoreType.DMA((4,))],
        flops=50 * heads * chunks * 2 * DH**3,
        space=pltpu.HBM,
    )
    other = swap(theirs)
    lead, local = call(
        functools.partial(read_kernel, heads, chunks),
        [shape((heads, tokens, DH), BF16), shape((heads, tokens, DH), F32)],
        [queries, keys, solved, before, rows],
        flops=3 * heads * chunks * 2 * DH**3,
    )
    first, pair = call(pair_kernel, [pair_shape, pair_shape], [place, mine, other])
    ring = [y_shift(pair, d) for d in (1, 2, 3)]
    *ring, lead, local = lax.optimization_barrier((*ring, lead, local))
    chip_before, whole, offset = call(
        ring_kernel,
        [shape((2, DH, 2 * DH), F32), pair_shape, shape((2, DH, DH), BF16)],
        [place, pair, *ring],
        scratch=[pltpu.VMEM((4, 2, DH, 2 * DH), BF16)],
    )
    shifts = [x_shift(whole, 1), x_shift(whole, 2), x_shift(offset, 3)]
    keep, send = call(
        state_kernel,
        [shape((2, DH, DH), BF16)] * 2,
        [place, first, chip_before, *shifts],
    )
    received = swap(send)
    block = tokens // 8
    width = heads * DH
    own, back, ahead = call(
        functools.partial(normed_kernel, heads),
        [shape((3 * block, width), BF16), shape((3 * block, width), BF16), shape((2 * block, width), BF16)],
        [place, lead, local, keep, received, norm_gain.reshape(1, -1)],
        scratch=[pltpu.VMEM((heads, DH, DH), BF16), pltpu.VMEM((tokens, width), BF16)],
        flops=2 * tokens * width * DH,
    )
    next_rows = z_shift(back, -1)
    across = [
        (i * 8 + z, (i ^ 1) * 8 + (z + (1 if i % 2 == 0 else -1)) % 8) for i in devices for z in range(8)
    ]
    other_rows = lax.ppermute(ahead, ("ctx", "head"), across)
    out_width = out_weight.shape[1]
    (total,) = call(
        own_kernel,
        [shape((3 * block, out_width), F32)],
        [own, out_weight],
        flops=2 * own.shape[0] * out_weight.size,
        limit=24,
    )
    next_weight, next_rows, other_rows, total = lax.optimization_barrier(
        (next_weight, next_rows, other_rows, total)
    )
    two, total, other_sum = call(
        next_kernel,
        [shape((block, out_width), BF16), shape((2 * block, out_width), F32), shape((2 * block, out_width), BF16)],
        [next_rows, other_rows, next_weight, total],
        flops=10 * block * out_weight.size,
        limit=24,
    )
    last_sum = swap(other_sum)
    two = z_shift(two, -2)
    kept, three = call(
        join_kernel,
        [shape((block, out_width), F32), shape((block, out_width), BF16)],
        [total, last_sum],
    )
    three = z_shift(three, 3)
    (out,) = call(add_kernel, [shape((block, out_width), BF16)], [kept, two, three])
    return out


def solution(mesh):
    return jax.shard_map(
        on_device,
        mesh=mesh,
        in_specs=(
            P("ctx", "head"),
            P("ctx", None, "head"),
            P("ctx", None, "head"),
            P("head", None, "ctx"),
            P("head", "ctx"),
            P("head"),
            P("head", None),
        ),
        out_specs=P(("ctx", "head"), None),
        check_vma=False,
    )
```

```python
import functools

import jax
import jax.numpy as jnp
from jax import lax
from jax.experimental import pallas as pl
from jax.experimental.pallas import tpu as pltpu
from jax.sharding import PartitionSpec as P

DH = 128
STEPS = 128
ROWS = STEPS // 2
F32 = jnp.float32
BF16 = jnp.bfloat16
NN = (((1,), (0,)), ((), ()))
NT = (((1,), (1,)), ((), ()))
TN = (((0,), (0,)), ((), ()))
VMEM = pl.BlockSpec(memory_space=pltpu.VMEM)
SMEM = pl.BlockSpec(memory_space=pltpu.SMEM)


def dot(a, b, dims=NN):
    return lax.dot_general(a, b, dims, preferred_element_type=F32)


def split(x):
    high = x.astype(BF16)
    return high, (x - high.astype(F32)).astype(BF16)


def dot_wide(a, b, dims=NN):
    a_high, a_low = split(a)
    b_high, b_low = split(b)
    return dot(a_high, b_high, dims) + (dot(a_high, b_low, dims) + dot(a_low, b_high, dims))


def dot_left(a, b, dims=NN):
    high, low = split(a)
    return dot(high, b, dims) + dot(low, b, dims)


def dot_right(a, b, dims=NN):
    high, low = split(b)
    return dot(a, high, dims) + dot(a, low, dims)


def iotas(rows, columns):
    return (
        lax.broadcasted_iota(jnp.int32, (rows, columns), 0),
        lax.broadcasted_iota(jnp.int32, (rows, columns), 1),
    )


def gate_sums(gates, betas):
    token, step = iotas(ROWS, STEPS)
    high = lax.Precision.HIGHEST
    upto = (2 * token <= step).astype(F32)
    sums = jnp.dot(gates, upto, precision=high, preferred_element_type=F32)
    even = (2 * token == step).astype(F32)
    odd = (2 * token + 1 == step).astype(F32)
    spread = jnp.dot(betas[0], even, precision=high, preferred_element_type=F32) + jnp.dot(
        betas[1], odd, precision=high, preferred_element_type=F32
    )
    return sums, spread


def unit_inverses(lowers):
    row, column = iotas(STEPS, STEPS)
    eye = (row == column).astype(F32)
    pairs = (row // 2 == column // 2) & (row > column)
    inverses = [eye - jnp.where(pairs, lower, 0.0) for lower in lowers]
    size = 2
    while size < STEPS:
        corner = (row // (2 * size) == column // (2 * size)) & (row // size > column // size)
        corners = [jnp.where(corner, lower, 0.0) for lower in lowers]
        parts = [split(inverse) for inverse in inverses]
        rights = [
            dot_right_parts(split(block), part) for block, part in zip(corners, parts)
        ]
        inverses = [
            inverse - dot_right_parts(part, split(right))
            for inverse, part, right in zip(inverses, parts, rights)
        ]
        size *= 2
    return inverses


def dot_right_parts(a, b):
    high, low = b
    top = jnp.concatenate([high, low], axis=1)
    bottom = jnp.concatenate([high, jnp.zeros_like(low)], axis=1)
    both = dot(jnp.concatenate(a, axis=1), jnp.concatenate([top, bottom], axis=0))
    return both[:, :STEPS] + both[:, STEPS:]


def local_kernel(
    heads, chunks, place_ref, k_hbm, v_hbm, beta_hbm, gate_hbm,
    mine_ref, theirs_ref, solved_ref, before_ref, rows_ref,
    k_ref, v_ref, beta_ref, gate_ref, arrived,
):
    core = place_ref[0]
    pairs = ((gate_hbm, gate_ref), (beta_hbm, beta_ref), (k_hbm, k_ref), (v_hbm, v_ref))
    copies = [pltpu.make_async_copy(a, b, arrived.at[i]) for i, (a, b) in enumerate(pairs)]
    for copy in copies:
        copy.start()
    for copy in copies[:3]:
        copy.wait()
    keys_all = k_ref.reshape(2 * k_ref.shape[0], k_ref.shape[2])
    values_all = v_ref.reshape(2 * v_ref.shape[0], v_ref.shape[2])
    row, column = iotas(STEPS, STEPS)
    eye = row == column
    strict = row > column

    def down(line):
        return jnp.sum(jnp.where(eye, line, 0.0), axis=1, keepdims=True)

    def across(stack):
        return jnp.sum(jnp.where(eye, stack, 0.0), axis=0, keepdims=True)

    work = []
    for c in range(chunks):
        at = pl.ds(c * ROWS, ROWS)
        gates = jnp.maximum(gate_ref[:, at], -200.0)
        sums, spread = gate_sums(gates, (beta_ref[:, 0, at], beta_ref[:, 1, at]))
        for h in range(heads):
            key = keys_all[pl.ds(c * STEPS, STEPS), pl.ds(h * DH, DH)]
            wide = key.astype(F32)
            norm = lax.rsqrt(jnp.sum(wide * wide, axis=1, keepdims=True) + 1e-06)
            norm_line = across(norm)
            total = sums[h : h + 1]
            total_down = down(total)
            beta_line = spread[h : h + 1]
            inner = dot(key, key, NT)
            decay = jnp.exp(jnp.minimum(total_down - total, 0.0))
            lower = jnp.where(strict, decay * (inner * norm) * (norm_line * beta_line), 0.0)
            rows_ref[h, c] = jnp.concatenate(
                [total, beta_line * norm_line, jnp.zeros((6, STEPS), F32)], axis=0
            )
            last = total[:, STEPS - 1 :]
            scale = jnp.exp(jnp.minimum(last - total_down, 0.0)) * down(beta_line) * norm
            work.append((c, h, key, lower, jnp.exp(total) * norm_line, scale, jnp.exp(last)))
    inverses = unit_inverses([w[3] for w in work])
    maps = {}
    copies[3].wait()
    for (c, h, key, _, carry, scale, fade), inverse in zip(work, inverses):
        value = values_all[pl.ds(c * STEPS, STEPS), pl.ds(h * DH, DH)]
        solved = jnp.concatenate(
            [dot_left(inverse * carry, key), dot_left(inverse, value)], axis=1
        )
        solved_ref[h, c] = solved.astype(BF16)
        moved = dot_right(key, scale * solved, TN)
        maps[c, h] = (
            jnp.where(eye, fade, 0.0) - moved[:, :DH],
            moved[:, DH:],
        )
    for h in range(heads):
        joined = jnp.concatenate(maps[0, h], axis=1)
        for c in range(1, chunks):
            before_ref[h, c - 1] = joined.astype(BF16)
            step_map, step_offset = maps[c, h]
            moved = dot_wide(step_map, joined)
            joined = jnp.concatenate([moved[:, :DH], moved[:, DH:] + step_offset], axis=1)
        result = joined.astype(BF16)

        @pl.when(core == h // 2)
        def _(result=result, h=h):
            mine_ref[h % 2] = result

        @pl.when(core != h // 2)
        def _(result=result, h=h):
            theirs_ref[h % 2] = result


def read_kernel(heads, chunks, q_ref, k_ref, solved_ref, before_ref, rows_ref, lead_ref, local_ref):
    keys_all = k_ref.reshape(2 * k_ref.shape[0], k_ref.shape[2])
    token, step = iotas(ROWS, STEPS)
    for h in range(heads):
        for c in range(chunks):
            query = q_ref[pl.ds(c * ROWS, ROWS), pl.ds(h * DH, DH)]
            key = keys_all[pl.ds(c * STEPS, STEPS), pl.ds(h * DH, DH)]
            lines = rows_ref[h, c]
            total, weight = lines[0:1], lines[1:2]
            at_token = jnp.sum(jnp.where(step == 2 * token, total, 0.0), axis=1, keepdims=True)
            visible = 2 * token + 1 >= step
            decay = jnp.exp(jnp.minimum(at_token - total, 0.0))
            scores = jnp.where(visible, dot(query, key, NT) * decay * weight, 0.0)
            seen = dot(scores.astype(BF16), solved_ref[h, c])
            lead = jnp.exp(at_token) * query.astype(F32) - seen[:, :DH]
            local = seen[:, DH:]
            if c:
                moved = dot(lead.astype(BF16), before_ref[h, c - 1])
                lead = moved[:, :DH]
                local = local + moved[:, DH:]
            lead_ref[h, pl.ds(c * ROWS, ROWS)] = lead.astype(BF16)
            local_ref[h, pl.ds(c * ROWS, ROWS)] = local


def pair_kernel(place_ref, mine_ref, other_ref, first_ref, pair_ref):
    core = place_ref[0]
    for h in range(2):
        mine, other = mine_ref[h].astype(F32), other_ref[h].astype(F32)
        first = jnp.where(core == 0, mine, other).astype(BF16)
        second = jnp.where(core == 0, other, mine)
        first_ref[h] = first
        moved = dot(second[:, :DH].astype(BF16), first)
        pair_ref[h] = jnp.concatenate(
            [moved[:, :DH], moved[:, DH:] + second[:, DH:]], axis=1
        ).astype(BF16)


def ring_kernel(place_ref, own_ref, one_ref, two_ref, three_ref, before_ref, whole_ref, offset_ref, slots):
    y = place_ref[1]
    for back, ref in enumerate((own_ref, one_ref, two_ref, three_ref)):
        slots[lax.rem(y - back + 4, 4)] = ref[...]
    row, column = iotas(DH, 2 * DH)
    nothing = (row == column).astype(F32)
    joined = [slots[0, h].astype(F32) for h in range(2)]
    before = [jnp.where(y == 1, joined[h], nothing) for h in range(2)]
    for k in range(1, 4):
        for h in range(2):
            step = slots[k, h]
            moved = dot_right(step[:, :DH], joined[h])
            joined[h] = jnp.concatenate(
                [moved[:, :DH], moved[:, DH:] + step[:, DH:].astype(F32)], axis=1
            )
            if k < 3:
                before[h] = jnp.where(y == k + 1, joined[h], before[h])
    for h in range(2):
        before_ref[h] = before[h]
        whole_ref[h] = joined[h].astype(BF16)
        offset_ref[h] = joined[h][:, DH:].astype(BF16)


def state_kernel(place_ref, first_ref, before_ref, one_ref, two_ref, three_ref, keep_ref, send_ref):
    core = place_ref[0]
    for h in range(2):
        state = three_ref[h].astype(F32)
        for ref in (two_ref, one_ref):
            state = dot_right(ref[h, :, :DH], state) + ref[h, :, DH:].astype(F32)
        chip = dot_wide(before_ref[h, :, :DH], state) + before_ref[h, :, DH:]
        later = dot_right(first_ref[h, :, :DH], chip) + first_ref[h, :, DH:].astype(F32)
        keep_ref[h] = jnp.where(core == 0, chip, later).astype(BF16)
        send_ref[h] = jnp.where(core == 0, later, chip).astype(BF16)


def normed_kernel(
    heads, place_ref, lead_ref, local_ref, keep_ref, other_ref, gain_ref,
    own_ref, back_ref, ahead_ref, states, normed,
):
    core, z = place_ref[0], place_ref[3]
    way = 1 - 2 * core
    states[pl.ds(core * 2, 2)] = keep_ref[...]
    states[pl.ds((1 - core) * 2, 2)] = other_ref[...]
    for h in range(heads):
        read = dot(lead_ref[h], states[h]) + local_ref[h]
        scale = lax.rsqrt(jnp.mean(read * read, axis=1, keepdims=True) + 1e-06)
        lanes = pl.ds(h * DH, DH)
        normed[:, lanes] = (read * scale * gain_ref[:, lanes]).astype(BF16)
    block = own_ref.shape[0] // 3
    for ref, offsets in ((own_ref, (0, 3, -2)), (back_ref, (-1, 2, -3)), (ahead_ref, (1, 4))):
        for i, offset in enumerate(offsets):
            at = lax.rem(z + way * offset + 8, 8) * block
            ref[pl.ds(i * block, block)] = normed[pl.ds(pl.multiple_of(at, block), block)]


def columns(ref, width=512):
    return [pl.ds(j, width) for j in range(0, ref.shape[1], width)]


def own_kernel(rows_ref, weight_ref, sum_ref):
    rows = rows_ref[...]
    for at in columns(sum_ref):
        sum_ref[:, at] = dot(rows, weight_ref[:, at])


def next_kernel(
    place_ref, next_ref, other_ref, near_ref, far_ref, last_ref, sum_ref, two_ref, rest_ref, other_sum_ref
):
    colour = lax.rem(place_ref[1] + place_ref[2], 2)
    part = near_ref.shape[1]
    next_rows, other_rows = next_ref[...], other_ref[...]
    kept = rest_ref.shape[0]
    for ref, skip in ((near_ref, colour * part), (far_ref, (1 - colour) * part), (last_ref, 2 * part)):
        for at in columns(ref):
            weights = ref[:, at]
            to = pl.ds(pl.multiple_of(skip + at.start, at.size), at.size)
            total = sum_ref[:, to] + dot(next_rows, weights)
            rest_ref[:, to] = total[:kept]
            two_ref[:, to] = total[kept:].astype(BF16)
            other_sum_ref[:, to] = dot(other_rows, weights).astype(BF16)


def join_kernel(sum_ref, last_ref, keep_ref, three_ref):
    total = sum_ref[...] + last_ref[...].astype(F32)
    kept = keep_ref.shape[0]
    keep_ref[...] = total[:kept]
    three_ref[...] = total[kept:].astype(BF16)


def add_kernel(keep_ref, two_ref, three_ref, out_ref):
    out_ref[...] = (keep_ref[...] + (two_ref[...].astype(F32) + three_ref[...].astype(F32))).astype(BF16)


def call(kernel, outs, args, scratch=(), flops=0, limit=16, spaces={}):
    moved = sum(a.size * a.dtype.itemsize for a in (*args, *outs))
    specs = [
        SMEM if a.dtype == jnp.int32 else pl.BlockSpec(memory_space=spaces.get(i, pltpu.VMEM))
        for i, a in enumerate(args)
    ]
    return pl.pallas_call(
        kernel,
        out_shape=tuple(outs),
        in_specs=specs,
        out_specs=tuple(VMEM for _ in outs),
        scratch_shapes=list(scratch),
        compiler_params=pltpu.CompilerParams(vmem_limit_bytes=limit * 2**20),
        cost_estimate=pl.CostEstimate(flops=flops, bytes_accessed=moved, transcendentals=0),
    )(*args)


def on_device(queries, keys, values, beta, log_gate, norm_gain, out_weight):
    heads = beta.shape[0]
    tokens = queries.shape[0]
    chunks = tokens // ROWS
    shape = jax.ShapeDtypeStruct
    ctx = lax.axis_index("ctx")
    head = lax.axis_index("head")
    place = jnp.stack([ctx % 2, (ctx // 2) % 4, ctx // 8, head]).astype(jnp.int32)
    devices = range(32)

    def y_shift(block, d):
        route = [(i, (i // 8) * 8 + ((i // 2 + d) % 4) * 2 + i % 2) for i in devices]
        return lax.ppermute(block, "ctx", route)

    def x_shift(block, d):
        return lax.ppermute(block, "ctx", [(i, i + 8 * d) for i in devices if i + 8 * d < 32])

    def swap(block):
        return lax.ppermute(block, "ctx", [(i, i ^ 1) for i in devices])

    def z_shift(block, d):
        route = [
            (i * 8 + z, i * 8 + (z + (d if i % 2 == 0 else -d)) % 8) for i in devices for z in range(8)
        ]
        return lax.ppermute(block, ("ctx", "head"), route)

    out_width = out_weight.shape[1]
    part = out_width // 4
    colour = (ctx // 8 + ctx // 2) % 2
    shared = lax.dynamic_slice(out_weight, (0, colour * part), (out_weight.shape[0], part))
    near = z_shift(shared, -1)
    pair_shape = shape((2, DH, 2 * DH), BF16)
    mine, theirs, solved, before, rows = call(
        functools.partial(local_kernel, heads, chunks),
        [
            pair_shape,
            pair_shape,
            shape((heads, chunks, STEPS, 2 * DH), BF16),
            shape((heads, chunks - 1, DH, 2 * DH), BF16),
            shape((heads, chunks, 8, STEPS), F32),
        ],
        [place, *(pltpu.with_memory_space_constraint(a, pltpu.HBM) for a in (keys, values, beta, log_gate))],
        scratch=[pltpu.VMEM(a.shape, a.dtype) for a in (keys, values, beta, log_gate)]
        + [pltpu.SemaphoreType.DMA((4,))],
        flops=50 * heads * chunks * 2 * DH**3,
        spaces=dict.fromkeys(range(1, 5), pltpu.HBM),
    )
    other = swap(theirs)
    lead, local = call(
        functools.partial(read_kernel, heads, chunks),
        [shape((heads, tokens, DH), BF16), shape((heads, tokens, DH), F32)],
        [queries, keys, solved, before, rows],
        flops=3 * heads * chunks * 2 * DH**3,
    )
    first, pair = call(pair_kernel, [pair_shape, pair_shape], [place, mine, other])
    ring = [y_shift(pair, d) for d in (1, 2, 3)]
    weight, rows = lax.optimization_barrier((out_weight, rows))
    rest, near, pair = lax.optimization_barrier((weight[:, 2 * part :], near, pair))
    rest = z_shift(rest, -1)
    sideways = [
        (i, ((i // 8 + (3 if i % 2 == 0 else 1)) % 4) * 8 + i % 8) for i in devices
    ]
    far = lax.ppermute(near, "ctx", sideways)
    *ring, lead, local = lax.optimization_barrier((*ring, lead, local))
    chip_before, whole, offset = call(
        ring_kernel,
        [shape((2, DH, 2 * DH), F32), pair_shape, shape((2, DH, DH), BF16)],
        [place, pair, *ring],
        scratch=[pltpu.VMEM((4, 2, DH, 2 * DH), BF16)],
    )
    shifts = [x_shift(whole, 1), x_shift(whole, 2), x_shift(offset, 3)]
    keep, send = call(
        state_kernel,
        [shape((2, DH, DH), BF16)] * 2,
        [place, first, chip_before, *shifts],
    )
    received = swap(send)
    block = tokens // 8
    width = heads * DH
    own, back, ahead = call(
        functools.partial(normed_kernel, heads),
        [shape((3 * block, width), BF16), shape((3 * block, width), BF16), shape((2 * block, width), BF16)],
        [place, lead, local, keep, received, norm_gain.reshape(1, -1)],
        scratch=[pltpu.VMEM((heads, DH, DH), BF16), pltpu.VMEM((tokens, width), BF16)],
        flops=2 * tokens * width * DH,
    )
    next_rows = z_shift(back, -1)
    across = [
        (i * 8 + z, (i ^ 1) * 8 + (z + (1 if i % 2 == 0 else -1)) % 8) for i in devices for z in range(8)
    ]
    other_rows = lax.ppermute(ahead, ("ctx", "head"), across)
    out_width = out_weight.shape[1]
    (total,) = call(
        own_kernel,
        [shape((3 * block, out_width), F32)],
        [own, out_weight],
        flops=2 * own.shape[0] * out_weight.size,
        limit=24,
    )
    rest, far, next_rows, other_rows, total = lax.optimization_barrier(
        (rest, far, next_rows, other_rows, total)
    )
    two, total, other_sum = call(
        next_kernel,
        [shape((block, out_width), BF16), shape((2 * block, out_width), F32), shape((2 * block, out_width), BF16)],
        [place, next_rows, other_rows, near, far, rest, total],
        flops=10 * block * out_weight.size,
        limit=24,
    )
    last_sum = swap(other_sum)
    two = z_shift(two, -2)
    kept, three = call(
        join_kernel,
        [shape((block, out_width), F32), shape((block, out_width), BF16)],
        [total, last_sum],
    )
    three = z_shift(three, 3)
    (out,) = call(add_kernel, [shape((block, out_width), BF16)], [kept, two, three])
    return out


def solution(mesh):
    return jax.shard_map(
        on_device,
        mesh=mesh,
        in_specs=(
            P("ctx", "head"),
            P("ctx", None, "head"),
            P("ctx", None, "head"),
            P("head", None, "ctx"),
            P("head", "ctx"),
            P("head"),
            P("head", None),
        ),
        out_specs=P(("ctx", "head"), None),
        check_vma=False,
    )
```

```python
import functools

import jax
import jax.numpy as jnp
from jax import lax
from jax.experimental import pallas as pl
from jax.experimental.pallas import tpu as pltpu
from jax.sharding import PartitionSpec as P

DH = 128
STEPS = 128
ROWS = STEPS // 2
F32 = jnp.float32
BF16 = jnp.bfloat16
NN = (((1,), (0,)), ((), ()))
NT = (((1,), (1,)), ((), ()))
TN = (((0,), (0,)), ((), ()))
VMEM = pl.BlockSpec(memory_space=pltpu.VMEM)
SMEM = pl.BlockSpec(memory_space=pltpu.SMEM)


def dot(a, b, dims=NN):
    return lax.dot_general(a, b, dims, preferred_element_type=F32)


def split(x):
    high = x.astype(BF16)
    return high, (x - high.astype(F32)).astype(BF16)


def dot_wide(a, b, dims=NN):
    a_high, a_low = split(a)
    b_high, b_low = split(b)
    return dot(a_high, b_high, dims) + (dot(a_high, b_low, dims) + dot(a_low, b_high, dims))


def dot_left(a, b, dims=NN):
    high, low = split(a)
    return dot(high, b, dims) + dot(low, b, dims)


def dot_right(a, b, dims=NN):
    high, low = split(b)
    return dot(a, high, dims) + dot(a, low, dims)


def iotas(rows, columns):
    return (
        lax.broadcasted_iota(jnp.int32, (rows, columns), 0),
        lax.broadcasted_iota(jnp.int32, (rows, columns), 1),
    )


def dot_exact(x, ones):
    high, low = split(x)
    least = (x - high.astype(F32) - low.astype(F32)).astype(BF16)
    return dot(high, ones) + (dot(low, ones) + dot(least, ones))


def gate_sums(gates, betas):
    token, step = iotas(ROWS, STEPS)
    sums = dot_exact(gates, (2 * token <= step).astype(BF16))
    even = dot_exact(betas[0], (2 * token == step).astype(BF16))
    odd = dot_exact(betas[1], (2 * token + 1 == step).astype(BF16))
    return sums, even + odd


def unit_inverses(lowers):
    row, column = iotas(STEPS, STEPS)
    eye = (row == column).astype(F32)
    pairs = (row // 2 == column // 2) & (row > column)
    inverses = [eye - jnp.where(pairs, lower, 0.0) for lower in lowers]
    lowers = [split(lower) for lower in lowers]
    size = 2
    while size < STEPS:
        corner = (row // (2 * size) == column // (2 * size)) & (row // size > column // size)
        corner = corner.astype(BF16)
        parts = [split(inverse) for inverse in inverses]
        halved = size >= 16
        pick = functools.partial(lower_rows, size) if halved else lambda x: x
        kept = pick(corner)
        rights = [
            dot_right_parts([pick(x) * kept for x in lower], part) for lower, part in zip(lowers, parts)
        ]
        rights = [split(right) for right in rights]
        if halved:
            rights = [[spread_rows(size, x) for x in right] for right in rights]
        changes = [
            dot_right_parts([pick(x) for x in part], right) for part, right in zip(parts, rights)
        ]
        if halved:
            changes = [spread_rows(size, change) for change in changes]
        inverses = [inverse - change for inverse, change in zip(inverses, changes)]
        size *= 2
    return inverses


def lower_rows(size, x):
    return jnp.concatenate([x[i : i + size] for i in range(size, STEPS, 2 * size)], axis=0)


def spread_rows(size, x):
    blocks = []
    for i in range(0, STEPS // 2, size):
        block = x[i : i + size]
        blocks += [jnp.zeros_like(block), block]
    return jnp.concatenate(blocks, axis=0)


def dot_right_parts(a, b):
    high, low = b
    top = jnp.concatenate([high, low], axis=1)
    bottom = jnp.concatenate([high, jnp.zeros_like(low)], axis=1)
    both = dot(jnp.concatenate(a, axis=1), jnp.concatenate([top, bottom], axis=0))
    return both[:, :STEPS] + both[:, STEPS:]


def local_kernel(
    heads, chunks, place_ref, k_hbm, v_hbm, beta_hbm, gate_hbm,
    mine_ref, theirs_ref, solved_ref, before_ref, rows_ref,
    k_ref, v_ref, beta_ref, gate_ref, arrived,
):
    core = place_ref[0]
    pairs = ((gate_hbm, gate_ref), (beta_hbm, beta_ref), (k_hbm, k_ref), (v_hbm, v_ref))
    copies = [pltpu.make_async_copy(a, b, arrived.at[i]) for i, (a, b) in enumerate(pairs)]
    for copy in copies:
        copy.start()
    for copy in copies[:3]:
        copy.wait()
    keys_all = k_ref.reshape(2 * k_ref.shape[0], k_ref.shape[2])
    values_all = v_ref.reshape(2 * v_ref.shape[0], v_ref.shape[2])
    row, column = iotas(STEPS, STEPS)
    eye = row == column
    strict = row > column

    def down(line):
        return jnp.sum(jnp.where(eye, line, 0.0), axis=1, keepdims=True)

    def across(stack):
        return jnp.sum(jnp.where(eye, stack, 0.0), axis=0, keepdims=True)

    def by_chunk(lines):
        return jnp.concatenate([lines[:, c * ROWS : (c + 1) * ROWS] for c in range(chunks)], axis=0)

    gates = by_chunk(jnp.maximum(gate_ref[...], -200.0))
    all_sums, all_spread = gate_sums(gates, (by_chunk(beta_ref[:, 0, :]), by_chunk(beta_ref[:, 1, :])))
    work = []
    for c in range(chunks):
        sums = all_sums[c * heads : (c + 1) * heads]
        spread = all_spread[c * heads : (c + 1) * heads]
        for h in range(heads):
            key = keys_all[pl.ds(c * STEPS, STEPS), pl.ds(h * DH, DH)]
            wide = key.astype(F32)
            norm = lax.rsqrt(jnp.sum(wide * wide, axis=1, keepdims=True) + 1e-06)
            norm_line = across(norm)
            total = sums[h : h + 1]
            total_down = down(total)
            beta_line = spread[h : h + 1]
            inner = dot(key, key, NT)
            decay = jnp.exp(jnp.minimum(total_down - total, 0.0))
            lower = jnp.where(strict, decay * (inner * norm) * (norm_line * beta_line), 0.0)
            rows_ref[h, c] = jnp.concatenate(
                [total, beta_line * norm_line, jnp.zeros((6, STEPS), F32)], axis=0
            )
            last = total[:, STEPS - 1 :]
            scale = jnp.exp(jnp.minimum(last - total_down, 0.0)) * down(beta_line) * norm
            work.append((c, h, key, lower, jnp.exp(total) * norm_line, scale, jnp.exp(last)))
    inverses = unit_inverses([w[3] for w in work])
    maps = {}
    copies[3].wait()
    for (c, h, key, _, carry, scale, fade), inverse in zip(work, inverses):
        value = values_all[pl.ds(c * STEPS, STEPS), pl.ds(h * DH, DH)]
        solved = jnp.concatenate(
            [dot_left(inverse * carry, key), dot_left(inverse, value)], axis=1
        )
        solved_ref[h, c] = solved.astype(BF16)
        moved = dot_right(key, scale * solved, TN)
        maps[c, h] = (
            jnp.where(eye, fade, 0.0) - moved[:, :DH],
            moved[:, DH:],
        )
    joined = [jnp.concatenate(maps[0, h], axis=1) for h in range(heads)]
    for c in range(1, chunks):
        for h in range(heads):
            before_ref[h, c - 1] = joined[h].astype(BF16)
        moved = [dot_wide(maps[c, h][0], joined[h]) for h in range(heads)]
        joined = [
            jnp.concatenate([m[:, :DH], m[:, DH:] + maps[c, h][1]], axis=1) for h, m in enumerate(moved)
        ]
    for h in range(heads):
        result = joined[h].astype(BF16)

        @pl.when(core == h // 2)
        def _(result=result, h=h):
            mine_ref[h % 2] = result

        @pl.when(core != h // 2)
        def _(result=result, h=h):
            theirs_ref[h % 2] = result


def read_kernel(heads, chunks, q_ref, k_ref, solved_ref, before_ref, rows_ref, lead_ref, local_ref):
    keys_all = k_ref.reshape(2 * k_ref.shape[0], k_ref.shape[2])
    token, step = iotas(ROWS, STEPS)
    for h in range(heads):
        for c in range(chunks):
            query = q_ref[pl.ds(c * ROWS, ROWS), pl.ds(h * DH, DH)]
            key = keys_all[pl.ds(c * STEPS, STEPS), pl.ds(h * DH, DH)]
            lines = rows_ref[h, c]
            total, weight = lines[0:1], lines[1:2]
            at_token = jnp.sum(jnp.where(step == 2 * token, total, 0.0), axis=1, keepdims=True)
            visible = 2 * token + 1 >= step
            decay = jnp.exp(jnp.minimum(at_token - total, 0.0))
            scores = jnp.where(visible, dot(query, key, NT) * decay * weight, 0.0)
            seen = dot(scores.astype(BF16), solved_ref[h, c])
            lead = jnp.exp(at_token) * query.astype(F32) - seen[:, :DH]
            local = seen[:, DH:]
            if c:
                moved = dot(lead.astype(BF16), before_ref[h, c - 1])
                lead = moved[:, :DH]
                local = local + moved[:, DH:]
            lead_ref[h, pl.ds(c * ROWS, ROWS)] = lead.astype(BF16)
            local_ref[h, pl.ds(c * ROWS, ROWS)] = local


def pair_kernel(place_ref, mine_ref, other_ref, first_ref, pair_ref):
    core = place_ref[0]
    for h in range(2):
        mine, other = mine_ref[h].astype(F32), other_ref[h].astype(F32)
        first = jnp.where(core == 0, mine, other).astype(BF16)
        second = jnp.where(core == 0, other, mine)
        first_ref[h] = first
        moved = dot(second[:, :DH].astype(BF16), first)
        pair_ref[h] = jnp.concatenate(
            [moved[:, :DH], moved[:, DH:] + second[:, DH:]], axis=1
        ).astype(BF16)


def ring_kernel(place_ref, own_ref, one_ref, two_ref, three_ref, before_ref, whole_ref, offset_ref, slots):
    y = place_ref[1]
    for back, ref in enumerate((own_ref, one_ref, two_ref, three_ref)):
        slots[lax.rem(y - back + 4, 4)] = ref[...]
    row, column = iotas(DH, 2 * DH)
    nothing = (row == column).astype(F32)
    joined = [slots[0, h].astype(F32) for h in range(2)]
    before = [jnp.where(y == 1, joined[h], nothing) for h in range(2)]
    for k in range(1, 4):
        for h in range(2):
            step = slots[k, h]
            moved = dot_right(step[:, :DH], joined[h])
            joined[h] = jnp.concatenate(
                [moved[:, :DH], moved[:, DH:] + step[:, DH:].astype(F32)], axis=1
            )
            if k < 3:
                before[h] = jnp.where(y == k + 1, joined[h], before[h])
    for h in range(2):
        before_ref[h] = before[h]
        whole_ref[h] = joined[h].astype(BF16)
        offset_ref[h] = joined[h][:, DH:].astype(BF16)


def state_kernel(place_ref, first_ref, before_ref, one_ref, two_ref, three_ref, keep_ref, send_ref):
    core = place_ref[0]
    for h in range(2):
        state = three_ref[h].astype(F32)
        for ref in (two_ref, one_ref):
            state = dot_right(ref[h, :, :DH], state) + ref[h, :, DH:].astype(F32)
        chip = dot_wide(before_ref[h, :, :DH], state) + before_ref[h, :, DH:]
        later = dot_right(first_ref[h, :, :DH], chip) + first_ref[h, :, DH:].astype(F32)
        keep_ref[h] = jnp.where(core == 0, chip, later).astype(BF16)
        send_ref[h] = jnp.where(core == 0, later, chip).astype(BF16)


def normed_kernel(
    heads, place_ref, lead_ref, local_ref, keep_ref, other_ref, gain_ref,
    own_ref, back_ref, ahead_ref, states, normed,
):
    core, z = place_ref[0], place_ref[3]
    way = 1 - 2 * core
    states[pl.ds(core * 2, 2)] = keep_ref[...]
    states[pl.ds((1 - core) * 2, 2)] = other_ref[...]
    for h in range(heads):
        read = dot(lead_ref[h], states[h]) + local_ref[h]
        scale = lax.rsqrt(jnp.mean(read * read, axis=1, keepdims=True) + 1e-06)
        lanes = pl.ds(h * DH, DH)
        normed[:, lanes] = (read * scale * gain_ref[:, lanes]).astype(BF16)
    block = own_ref.shape[0] // 3
    for ref, offsets in ((own_ref, (0, 3, -2)), (back_ref, (-1, 2, -3)), (ahead_ref, (1, 4))):
        for i, offset in enumerate(offsets):
            at = lax.rem(z + way * offset + 8, 8) * block
            ref[pl.ds(i * block, block)] = normed[pl.ds(pl.multiple_of(at, block), block)]


def columns(ref, width=256):
    return [pl.ds(j, width) for j in range(0, ref.shape[1], width)]


def own_kernel(rows_ref, weight_ref, sum_ref):
    rows = rows_ref[...]
    for at in columns(sum_ref):
        sum_ref[:, at] = dot(rows, weight_ref[:, at])


def next_kernel(
    place_ref, next_ref, other_ref, near_ref, far_ref, last_ref, sum_ref, two_ref, rest_ref, other_sum_ref
):
    colour = lax.rem(place_ref[1] + place_ref[2], 2)
    part = near_ref.shape[1]
    next_rows, other_rows = next_ref[...], other_ref[...]
    kept = rest_ref.shape[0]
    for ref, skip in ((near_ref, colour * part), (far_ref, (1 - colour) * part), (last_ref, 2 * part)):
        for at in columns(ref):
            weights = ref[:, at]
            to = pl.ds(pl.multiple_of(skip + at.start, at.size), at.size)
            total = sum_ref[:, to] + dot(next_rows, weights)
            rest_ref[:, to] = total[:kept]
            two_ref[:, to] = total[kept:].astype(BF16)
            other_sum_ref[:, to] = dot(other_rows, weights).astype(BF16)


def join_kernel(sum_ref, last_ref, keep_ref, three_ref):
    total = sum_ref[...] + last_ref[...].astype(F32)
    kept = keep_ref.shape[0]
    keep_ref[...] = total[:kept]
    three_ref[...] = total[kept:].astype(BF16)


def add_kernel(keep_ref, two_ref, three_ref, out_ref):
    out_ref[...] = (keep_ref[...] + (two_ref[...].astype(F32) + three_ref[...].astype(F32))).astype(BF16)


def call(kernel, outs, args, scratch=(), flops=0, limit=16, spaces={}):
    moved = sum(a.size * a.dtype.itemsize for a in (*args, *outs))
    specs = [
        SMEM if a.dtype == jnp.int32 else pl.BlockSpec(memory_space=spaces.get(i, pltpu.VMEM))
        for i, a in enumerate(args)
    ]
    return pl.pallas_call(
        kernel,
        out_shape=tuple(outs),
        in_specs=specs,
        out_specs=tuple(VMEM for _ in outs),
        scratch_shapes=list(scratch),
        compiler_params=pltpu.CompilerParams(vmem_limit_bytes=limit * 2**20),
        cost_estimate=pl.CostEstimate(flops=flops, bytes_accessed=moved, transcendentals=0),
    )(*args)


def on_device(queries, keys, values, beta, log_gate, norm_gain, out_weight):
    heads = beta.shape[0]
    tokens = queries.shape[0]
    chunks = tokens // ROWS
    shape = jax.ShapeDtypeStruct
    ctx = lax.axis_index("ctx")
    head = lax.axis_index("head")
    place = jnp.stack([ctx % 2, (ctx // 2) % 4, ctx // 8, head]).astype(jnp.int32)
    devices = range(32)

    def y_shift(block, d):
        route = [(i, (i // 8) * 8 + ((i // 2 + d) % 4) * 2 + i % 2) for i in devices]
        return lax.ppermute(block, "ctx", route)

    def x_shift(block, d):
        return lax.ppermute(block, "ctx", [(i, i + 8 * d) for i in devices if i + 8 * d < 32])

    def swap(block):
        return lax.ppermute(block, "ctx", [(i, i ^ 1) for i in devices])

    def z_shift(block, d):
        route = [
            (i * 8 + z, i * 8 + (z + (d if i % 2 == 0 else -d)) % 8) for i in devices for z in range(8)
        ]
        return lax.ppermute(block, ("ctx", "head"), route)

    out_width = out_weight.shape[1]
    part = out_width * 3 // 16
    colour = (ctx // 8 + ctx // 2) % 2
    shared = lax.dynamic_slice(out_weight, (0, colour * part), (out_weight.shape[0], part))
    near = z_shift(shared, -1)
    pair_shape = shape((2, DH, 2 * DH), BF16)
    mine, theirs, solved, before, rows = call(
        functools.partial(local_kernel, heads, chunks),
        [
            pair_shape,
            pair_shape,
            shape((heads, chunks, STEPS, 2 * DH), BF16),
            shape((heads, chunks - 1, DH, 2 * DH), BF16),
            shape((heads, chunks, 8, STEPS), F32),
        ],
        [place, *(pltpu.with_memory_space_constraint(a, pltpu.HBM) for a in (keys, values, beta, log_gate))],
        scratch=[pltpu.VMEM(a.shape, a.dtype) for a in (keys, values, beta, log_gate)]
        + [pltpu.SemaphoreType.DMA((4,))],
        flops=50 * heads * chunks * 2 * DH**3,
        spaces=dict.fromkeys(range(1, 5), pltpu.HBM),
    )
    other = swap(theirs)
    lead, local = call(
        functools.partial(read_kernel, heads, chunks),
        [shape((heads, tokens, DH), BF16), shape((heads, tokens, DH), F32)],
        [queries, keys, solved, before, rows],
        flops=3 * heads * chunks * 2 * DH**3,
    )
    first, pair = call(pair_kernel, [pair_shape, pair_shape], [place, mine, other])
    ring = [y_shift(pair, d) for d in (1, 2, 3)]
    weight, rows = lax.optimization_barrier((out_weight, rows))
    rest, near, pair = lax.optimization_barrier((weight[:, 2 * part :], near, pair))
    rest = z_shift(rest, -1)
    sideways = [
        (i, ((i // 8 + (3 if i % 2 == 0 else 1)) % 4) * 8 + i % 8) for i in devices
    ]
    far = lax.ppermute(near, "ctx", sideways)
    *ring, lead, local = lax.optimization_barrier((*ring, lead, local))
    chip_before, whole, offset = call(
        ring_kernel,
        [shape((2, DH, 2 * DH), F32), pair_shape, shape((2, DH, DH), BF16)],
        [place, pair, *ring],
        scratch=[pltpu.VMEM((4, 2, DH, 2 * DH), BF16)],
    )
    shifts = [x_shift(whole, 1), x_shift(whole, 2), x_shift(offset, 3)]
    keep, send = call(
        state_kernel,
        [shape((2, DH, DH), BF16)] * 2,
        [place, first, chip_before, *shifts],
    )
    received = swap(send)
    block = tokens // 8
    width = heads * DH
    own, back, ahead = call(
        functools.partial(normed_kernel, heads),
        [shape((3 * block, width), BF16), shape((3 * block, width), BF16), shape((2 * block, width), BF16)],
        [place, lead, local, keep, received, norm_gain.reshape(1, -1)],
        scratch=[pltpu.VMEM((heads, DH, DH), BF16), pltpu.VMEM((tokens, width), BF16)],
        flops=2 * tokens * width * DH,
    )
    next_rows = z_shift(back, -1)
    across = [
        (i * 8 + z, (i ^ 1) * 8 + (z + (1 if i % 2 == 0 else -1)) % 8) for i in devices for z in range(8)
    ]
    other_rows = lax.ppermute(ahead, ("ctx", "head"), across)
    out_width = out_weight.shape[1]
    (total,) = call(
        own_kernel,
        [shape((3 * block, out_width), F32)],
        [own, out_weight],
        flops=2 * own.shape[0] * out_weight.size,
        limit=24,
    )
    rest, far, next_rows, other_rows, total = lax.optimization_barrier(
        (rest, far, next_rows, other_rows, total)
    )
    two, total, other_sum = call(
        next_kernel,
        [shape((block, out_width), BF16), shape((2 * block, out_width), F32), shape((2 * block, out_width), BF16)],
        [place, next_rows, other_rows, near, far, rest, total],
        flops=10 * block * out_weight.size,
        limit=24,
    )
    last_sum = swap(other_sum)
    two = z_shift(two, -2)
    kept, three = call(
        join_kernel,
        [shape((block, out_width), F32), shape((block, out_width), BF16)],
        [total, last_sum],
    )
    three = z_shift(three, 3)
    (out,) = call(add_kernel, [shape((block, out_width), BF16)], [kept, two, three])
    return out


def solution(mesh):
    return jax.shard_map(
        on_device,
        mesh=mesh,
        in_specs=(
            P("ctx", "head"),
            P("ctx", None, "head"),
            P("ctx", None, "head"),
            P("head", None, "ctx"),
            P("head", "ctx"),
            P("head"),
            P("head", None),
        ),
        out_specs=P(("ctx", "head"), None),
        check_vma=False,
    )
```
